256 devices in a mesh: section: 16 (over x_hi, y, core), tm: 16 (over z, x_lo).
Axes of the slice: x: 4 (x_hi: 2, x_lo: 2; x = x_hi * 2 + x_lo), y: 4, z: 8, core: 2. Of those that a mesh axis runs over, the one named last changes fastest.
Arguments:
- fwd_input: bfloat16 [16, 2048, 1536], P('section', 'tm'), may hold values from -6 to 6
- saved_input: bfloat16 [16, 2048, 1536], P('section', 'tm'), may hold values from -6 to 6
- grad_in: bfloat16 [16, 2048, 1536], P('section', 'tm'), may hold values from -6 to 6
- gain: float32 [16, 1536], P('section'), may hold values from 0.25 to 1.75
- kernel: float32 [16, 31, 1536], P('section'), may hold values from -1 to 1
- w_out: bfloat16 [16, 1536, 1536], P('section', 'tm'), may hold values from -0.15625 to 0.15625
- lengths: int32 [32], replicated, may hold values from 1 to 2048, 49152 in all
- plan: int32 [16, 2], P('section'), may hold values from 0 to 31
Outputs:
- passed_activation: bfloat16 [16, 2048, 1536], P('section', 'tm')
- passed_gradient: bfloat16 [16, 2048, 1536], P('section', 'tm')
- weight_grad: float32 [16, 1536, 1536], P('section', 'tm')
- kernel_grad: float32 [16, 31, 1536], P('section')
- gain_grad: float32 [16, 1536], P('section')
The draws below stay inside these ranges and needn't reach their ends.
Inputs may be any that keep to these rules, and one draw needn't show every extreme that they name: `lengths`: 32 valid counts summing to 49152, the largest exactly 2048. `plan`: indices into lengths.
All inputs are finite; a program needn't handle non-finite values.
Results may differ from the reference program's by a relative error of at most 0.017.
Values may be sent and summed in bfloat16 or wider, within the bound.
No kernel may reach another device: no remote copies, remote signals or barrier semaphores. Data moves between devices by JAX's collectives and lax.ppermute only.
A program may use at most 64 MiB of HBM per device.

```python
import math
import jax
import jax.numpy as jnp
import numpy as np
from jax import lax

D = 1536
KW = 31
MICRO = 32
FRAMES_DEV = 128
FRAMES = 2048
SECTIONS = 16
N_TM = 16


def plant(entries, own_key, low, largest):
    longest = entries.shape.index(max(entries.shape))
    spots = []
    for shift in (0, 1):
        where = [jax.random.randint(jax.random.fold_in(own_key, axis), (), 0, length) for axis, length in enumerate(entries.shape)]
        where[longest] = (where[longest] + shift) % entries.shape[longest]
        spots.append(tuple(where))
    return entries.at[spots[0]].set(low).at[spots[1]].set(largest)


def levels(key, dims, cuts, low, top_value):
    level, own = 1.0, jax.random.fold_in(key, 6)
    for dim, shards_of in cuts:
        heights = jnp.exp(jax.random.uniform(jax.random.fold_in(own, dim), (shards_of,), jnp.float32, low / len(cuts), top_value / len(cuts)))
        level = level * jnp.repeat(heights, dims[dim] // shards_of).reshape([-1 if axis == dim else 1 for axis in range(len(dims))])
    return level


def length_profile(count, total, most, slope):
    loads = [(1 << 20) // math.isqrt(standing ** slope) + 1 for standing in range(2, count + 1)]
    rest, holding = total - most - (count - 1), [1] * (count - 1)
    while rest > 0:
        free = [i for i in range(count - 1) if holding[i] < most]
        whole, remaining = sum([loads[i] for i in free]), rest
        for i in free:
            more = min(most - holding[i], max(1, remaining * loads[i] // whole), rest)
            holding[i] = holding[i] + more
            rest = rest - more
    return np.array([most] + holding)


def ragged(stream_key, amount, total, bound, slope):
    if amount == 2:
        one = jax.random.randint(stream_key, (), max(1, total - bound), min(bound, total - 1) + 1)
        return jnp.stack([one, total - one])
    sizes = jnp.asarray(length_profile(amount, total, bound, slope), jnp.int32)
    pairs = (amount - 1) // 2
    donor, sink = sizes[1:1 + 2 * pairs:2], sizes[2:2 + 2 * pairs:2]
    slack = jnp.minimum(donor - 1, bound - sink)
    moved = jax.random.randint(jax.random.fold_in(stream_key, 1), (pairs,), 0, 1 << 20) % (slack + 1)
    sizes = sizes.at[1:1 + 2 * pairs:2].set(donor - moved).at[2:2 + 2 * pairs:2].set(sink + moved)
    return sizes[jax.random.permutation(jax.random.fold_in(stream_key, 2), amount)]


def normal_values(rng, dims, scale, bound, pieces=(), kind=jnp.bfloat16):
    drawn = jax.random.normal(rng, dims, jnp.float32) * scale
    if len(pieces) > 0:
        drawn = levels(rng, dims, pieces, -0.22, 0.18) * drawn
    return jnp.clip(drawn, min=-bound, max=bound).astype(kind)


def setup_inputs(seed: int = 0) -> dict:
    arg_keys = jax.random.split(jax.random.key(seed), 9)
    fwd_input = normal_values(arg_keys[0], (SECTIONS, FRAMES, D), 1.0, 6.0, ((0, 16), (1, 16)))
    saved_input = normal_values(arg_keys[1], (SECTIONS, FRAMES, D), 1.0, 6.0, ((0, 16), (1, 16)))
    grad_in = normal_values(arg_keys[2], (SECTIONS, FRAMES, D), 1.0, 6.0, ((0, 16), (1, 16)))
    gain = jnp.clip(1.0 + 0.15 * jax.random.normal(arg_keys[3], (SECTIONS, D), jnp.float32), 0.25, 1.75)
    kernel = normal_values(arg_keys[4], (SECTIONS, KW, D), KW ** -0.5, 1.0, ((0, 16),), jnp.float32)
    w_out = normal_values(arg_keys[5], (SECTIONS, D, D), D ** -0.5, 0.15625, ((0, 16), (1, 16)))
    lengths = ragged(arg_keys[6], MICRO, 3 * MICRO * FRAMES // 4, FRAMES, 0).astype(jnp.int32)
    plan = plant(jax.random.randint(arg_keys[7], (SECTIONS, 2), 0, MICRO), jax.random.fold_in(arg_keys[7], 1), 0, MICRO - 1).astype(jnp.int32)
    return {"fwd_input": fwd_input, "saved_input": saved_input, "grad_in": grad_in, "gain": gain, "kernel": kernel, "w_out": w_out, "lengths": lengths, "plan": plan}


def normalize(values):
    center = values - lax.optimization_barrier(jnp.mean(values, axis=-1, keepdims=True))
    inverse = lax.rsqrt(lax.optimization_barrier(jnp.mean(center * center, axis=-1, keepdims=True)) + 1e-05)
    return (center * inverse, inverse)

def swish_act(values):
    return values * jax.nn.sigmoid(values)

def conv_taps(padded, kernel_rows, frames):
    running = jnp.zeros((frames, padded.shape[1]), jnp.float32)
    for tap_index in range(KW):
        running = running + kernel_rows[tap_index] * padded[tap_index:tap_index + frames]
    return running

def section_step(section_items, lengths):
    fwd_rows, saved_rows, upstream, gain_row, kernel_rows, w_rows, plan_row = section_items
    margin = KW // 2
    factor = float(FRAMES) ** (-0.5)
    position = jnp.arange(FRAMES, dtype=jnp.int32)
    slot_ids = jnp.arange(MICRO, dtype=jnp.int32)
    fwd_len = jnp.sum(jnp.where(slot_ids == plan_row[0], lengths, 0))
    bwd_len = jnp.sum(jnp.where(slot_ids == plan_row[1], lengths, 0))
    fwd_mask = (position < fwd_len).astype(jnp.float32)[:, None]
    bwd_mask = (position < bwd_len).astype(jnp.float32)[:, None]
    fwd_float = fwd_rows.astype(jnp.float32)
    fwd_hat, unused_inverse = normalize(fwd_float)
    conv_fwd = (fwd_hat * gain_row * fwd_mask).astype(jnp.bfloat16)
    pad_fwd = jnp.pad(conv_fwd.astype(jnp.float32), ((margin, margin), (0, 0)))
    hidden_fwd = swish_act(conv_taps(pad_fwd, kernel_rows, FRAMES)).astype(jnp.bfloat16)
    output = (fwd_float + jnp.dot(hidden_fwd, w_rows, preferred_element_type=jnp.float32)).astype(jnp.bfloat16)
    saved_float = saved_rows.astype(jnp.float32)
    saved_hat, inverse = normalize(saved_float)
    conv_saved = (saved_hat * gain_row * bwd_mask).astype(jnp.bfloat16)
    pad_saved = jnp.pad(conv_saved.astype(jnp.float32), ((margin, margin), (0, 0)))
    mixed_saved = conv_taps(pad_saved, kernel_rows, FRAMES)
    hidden_saved = swish_act(mixed_saved).astype(jnp.bfloat16)
    hidden_grad = lax.dot_general(upstream, w_rows, (((1,), (1,)), ((), ())), preferred_element_type=jnp.float32)
    gate_sig = jax.nn.sigmoid(mixed_saved)
    conv_grad = (hidden_grad * (gate_sig + mixed_saved * gate_sig * (1.0 - gate_sig))).astype(jnp.bfloat16)
    grad_float = conv_grad.astype(jnp.float32)
    pad_grad = jnp.pad(grad_float, ((margin, margin), (0, 0)))
    input_grad = jnp.zeros((FRAMES, D), jnp.float32)
    for tap_index in range(KW):
        begin_at = 2 * margin - tap_index
        input_grad = input_grad + kernel_rows[tap_index] * pad_grad[begin_at:begin_at + FRAMES]
    kernel_grad = jnp.stack([lax.optimization_barrier(jnp.sum(grad_float * pad_saved[tap_index:tap_index + FRAMES], axis=0)) for tap_index in range(KW)]) * factor
    norm_grad = input_grad * bwd_mask
    gain_grad = lax.optimization_barrier(jnp.sum(norm_grad * saved_hat, axis=0)) * factor
    hat_grad = norm_grad * gain_row
    input_back = upstream.astype(jnp.float32) + inverse * (hat_grad - lax.optimization_barrier(jnp.mean(hat_grad, axis=-1, keepdims=True)) - saved_hat * lax.optimization_barrier(jnp.mean(hat_grad * saved_hat, axis=-1, keepdims=True)))
    hidden_blocks = hidden_saved.reshape(N_TM, FRAMES_DEV, D).astype(jnp.float32)
    upstream_blocks = upstream.reshape(N_TM, FRAMES_DEV, D).astype(jnp.float32)
    partial_sums = jnp.einsum('tfi,tfj->tij', hidden_blocks, upstream_blocks) * factor
    weight_grad = lax.optimization_barrier(jnp.sum(lax.optimization_barrier(partial_sums.astype(jnp.bfloat16)).astype(jnp.float32), axis=0))
    return (output, input_back.astype(jnp.bfloat16), weight_grad, kernel_grad, gain_grad)

def reference(fwd_input, saved_input, grad_in, gain, kernel, w_out, lengths, plan):

    def run_section(section_items):
        return section_step(section_items, lengths)
    outputs, backs, weight_grad, kernel_grad, gain_grad = lax.map(run_section, (fwd_input, saved_input, grad_in, gain, kernel, w_out, plan))
    blank = jnp.zeros((1, FRAMES, D), jnp.bfloat16)
    passed_activation = jnp.concatenate([blank, outputs[:-1]], axis=0)
    passed_gradient = jnp.concatenate([backs[1:], blank], axis=0)
    return (passed_activation, passed_gradient, weight_grad, kernel_grad, gain_grad)
```

```python
import jax
import jax.numpy as jnp
from jax import lax
from jax.sharding import Mesh
from jax.sharding import PartitionSpec as P

KW = 31
MARGIN = KW // 2
HALO = 16


def normalize(values):
    center = values - jnp.mean(values, axis=-1, keepdims=True)
    inverse = lax.rsqrt(jnp.mean(center * center, axis=-1, keepdims=True) + 1e-05)
    return (center * inverse, inverse)


def along(array, shift):
    pieces = lax.axis_size("z") * lax.axis_size("x")
    pairs = [(i, i + shift) for i in range(pieces) if 0 <= i + shift < pieces]
    return lax.ppermute(array, ("z", "x"), pairs)


def partner(array):
    return lax.ppermute(array, "x", [(0, 1), (1, 0)])


def from_behind(array, by):
    length = lax.axis_size("section")
    pairs = [(i, i + by) for i in range(length) if 0 <= i + by < length]
    return lax.ppermute(array, "section", pairs)


def conv_taps(padded, kernel_rows, frames, first):
    running = jnp.zeros((frames, padded.shape[-1]), jnp.float32)
    for tap in range(KW):
        running = running + kernel_rows[tap] * padded[first + tap : first + tap + frames]
    return running


def per_device(fwd_input, saved_input, grad_in, gain, kernel, w_out, lengths, plan):
    frames, width = fwd_input.shape[1:]
    depth = lax.axis_size("z")
    pieces = depth * lax.axis_size("x")
    side = lax.axis_index("x")
    rows = w_out.shape[1]
    half = rows * depth
    factor = float(frames * pieces) ** (-0.5)
    base = (lax.axis_index("z") * lax.axis_size("x") + side) * frames
    slot_ids = lax.iota(jnp.int32, lengths.shape[0])
    fwd_len = jnp.sum(jnp.where(slot_ids == plan[0, 0], lengths, 0))
    bwd_len = jnp.sum(jnp.where(slot_ids == plan[0, 1], lengths, 0))
    gain_row = gain[0]
    kernel_rows = kernel[0]
    fwd_rows = fwd_input[0]
    saved_rows = saved_input[0]
    upstream = grad_in[0]

    w_half = lax.all_gather(w_out[0], "z", axis=0, tiled=True)

    last = jnp.concatenate([saved_rows[-2 * HALO :], fwd_rows[-HALO:], upstream[-HALO:]])
    first = jnp.concatenate([saved_rows[: 2 * HALO], fwd_rows[:HALO], upstream[:HALO]])
    before = along(last, 1)
    after = along(first, -1)
    saved_ext = jnp.concatenate([before[: 2 * HALO], saved_rows, after[: 2 * HALO]])
    fwd_ext = jnp.concatenate([before[2 * HALO : 3 * HALO], fwd_rows, after[2 * HALO : 3 * HALO]])
    grad_ext = jnp.concatenate([before[3 * HALO :], upstream, after[3 * HALO :]])
    grad_other = partner(grad_ext)

    channel = lax.broadcasted_iota(jnp.int32, (width, half), 0)
    column = lax.broadcasted_iota(jnp.int32, (width, half), 1)
    natural = (column // rows) * (2 * rows) + column % rows
    pick_own = (channel == natural + side * rows).astype(jnp.bfloat16)
    pick_other = (channel == natural + (1 - side) * rows).astype(jnp.bfloat16)

    def positions(count, start):
        return (base + start + lax.iota(jnp.int32, count))[:, None]

    fwd_hat, _ = normalize(fwd_ext.astype(jnp.float32))
    fwd_mask = (positions(frames + 2 * HALO, -HALO) < fwd_len).astype(jnp.float32)
    conv_fwd = (fwd_hat * gain_row * fwd_mask).astype(jnp.bfloat16).astype(jnp.float32)
    saved_hat, inverse = normalize(saved_ext.astype(jnp.float32))
    saved_mask = (positions(frames + 4 * HALO, -2 * HALO) < bwd_len).astype(jnp.float32)
    conv_saved = (saved_hat * gain_row * saved_mask).astype(jnp.bfloat16).astype(jnp.float32)

    mixed_saved = conv_taps(conv_saved, kernel_rows, frames + 2 * HALO, HALO - MARGIN)
    gate = jax.nn.sigmoid(mixed_saved)
    hidden_saved = (mixed_saved * gate)[HALO : HALO + frames].astype(jnp.bfloat16)
    slope = gate + mixed_saved * gate * (1.0 - gate)
    mixed_fwd = conv_taps(conv_fwd, kernel_rows, frames, HALO - MARGIN)
    hidden_fwd = (mixed_fwd * jax.nn.sigmoid(mixed_fwd)).astype(jnp.bfloat16)

    def pick(array, matrix):
        return jnp.dot(array, matrix, preferred_element_type=jnp.float32).astype(jnp.bfloat16)

    saved_other = partner(pick(hidden_saved, pick_other))
    fwd_other = partner(pick(hidden_fwd, pick_other))
    saved_own = pick(hidden_saved, pick_own)
    fwd_own = pick(hidden_fwd, pick_own)

    def outer(left, right):
        return lax.dot_general(left, right, (((0,), (0,)), ((), ())), preferred_element_type=jnp.float32)

    partial_weight = (
        outer(
            jnp.concatenate([saved_own, saved_other]),
            jnp.concatenate([upstream, grad_other[HALO : HALO + frames]]),
        )
        * factor
    ).astype(jnp.bfloat16)
    weight_grad = lax.psum_scatter(
        lax.optimization_barrier(partial_weight), "z", scatter_dimension=0, tiled=True
    ).astype(jnp.float32)

    def back_dot(array):
        return lax.dot_general(
            array, w_half, (((1,), (1,)), ((), ())), preferred_element_type=jnp.float32
        ).astype(jnp.bfloat16)

    grad_for_other = back_dot(grad_other)
    grad_got = partner(grad_for_other)
    grad_own = back_dot(grad_ext)

    def forward_dot(array):
        return jnp.dot(array, w_half, preferred_element_type=jnp.float32)

    product_got = partner(forward_dot(fwd_other).astype(jnp.bfloat16))
    output = (
        fwd_rows.astype(jnp.float32) + (forward_dot(fwd_own) + product_got.astype(jnp.float32))
    ).astype(jnp.bfloat16)
    passed_activation = from_behind(output[None], 1)

    def place(array, matrix):
        return lax.dot_general(
            array, matrix, (((1,), (1,)), ((), ())), preferred_element_type=jnp.float32
        )

    hidden_grad = place(grad_own, pick_own) + place(grad_got, pick_other)
    conv_grad = (hidden_grad * slope).astype(jnp.bfloat16).astype(jnp.float32)
    input_grad = jnp.zeros((frames, width), jnp.float32)
    for tap in range(KW):
        begin = HALO + MARGIN - tap
        input_grad = input_grad + kernel_rows[tap] * conv_grad[begin : begin + frames]
    own_grad = conv_grad[HALO : HALO + frames]
    begin = 2 * HALO - MARGIN
    kernel_local = (
        jnp.stack(
            [
                jnp.sum(own_grad * conv_saved[begin + tap : begin + tap + frames], axis=0)
                for tap in range(KW)
            ]
        )
        * factor
    )
    total = kernel_local.astype(jnp.bfloat16)
    total = (total.astype(jnp.float32) + partner(total).astype(jnp.float32)).astype(jnp.bfloat16)
    step = 1
    while step < depth:
        got = lax.ppermute(total, "z", [(i, i ^ step) for i in range(depth)])
        kernel_grad = total.astype(jnp.float32) + got.astype(jnp.float32)
        total = kernel_grad.astype(jnp.bfloat16)
        step *= 2
    gain_grad = jnp.sum(kernel_rows * kernel_grad, axis=0) / gain_row

    own = slice(2 * HALO, 2 * HALO + frames)
    hat = saved_hat[own]
    hat_grad = input_grad * saved_mask[own] * gain_row
    input_back = upstream.astype(jnp.float32) + inverse[own] * (
        hat_grad
        - jnp.mean(hat_grad, axis=-1, keepdims=True)
        - hat * jnp.mean(hat_grad * hat, axis=-1, keepdims=True)
    )
    passed_gradient = from_behind(input_back.astype(jnp.bfloat16)[None], -1)
    return (
        passed_activation,
        passed_gradient,
        weight_grad[None],
        kernel_grad[None],
        gain_grad[None],
    )


def solution(mesh):
    sections, pieces = mesh.devices.shape
    folded = Mesh(mesh.devices.reshape(sections, pieces // 2, 2), ("section", "z", "x"))
    split = P("section", ("z", "x"), None)
    placed = (
        split,
        split,
        split,
        P("section", None),
        P("section", None, None),
        split,
        P(),
        P("section", None),
    )
    return jax.shard_map(
        per_device,
        mesh=folded,
        in_specs=placed,
        out_specs=(split, split, split, P("section", None, None), P("section", None)),
        check_vma=False,
    )
```

```python
import functools

import jax
import jax.numpy as jnp
from jax import lax
from jax.experimental import pallas as pl
from jax.experimental.pallas import tpu as pltpu
from jax.sharding import Mesh
from jax.sharding import PartitionSpec as P

KW = 31
MARGIN = KW // 2
HALO = 16
LANES = 128
ROWS = 16


VMEM = pl.BlockSpec(memory_space=pltpu.VMEM)
SMEM = pl.BlockSpec(memory_space=pltpu.SMEM)


def call(body, outs, in_specs, scratch=(), flops=0, size=0):
    return pl.pallas_call(
        body,
        out_shape=[jax.ShapeDtypeStruct(shape, kind) for shape, kind in outs],
        in_specs=in_specs,
        out_specs=[VMEM] * len(outs),
        scratch_shapes=list(scratch),
        compiler_params=pltpu.CompilerParams(vmem_limit_bytes=40 << 20),
        cost_estimate=pl.CostEstimate(flops=flops, bytes_accessed=size, transcendentals=0),
    )


def partner(array):
    return lax.ppermute(array, "x", [(0, 1), (1, 0)])


def from_behind(array, by):
    length = lax.axis_size("section")
    pairs = [(i, i + by) for i in range(length) if 0 <= i + by < length]
    return lax.ppermute(array, "section", pairs)


def divide(array, block):
    count = array.shape[1] // block
    pieces = [array[:, k * block : (k + 1) * block] for k in range(count)]
    return jnp.concatenate(pieces[0::2], axis=1), jnp.concatenate(pieces[1::2], axis=1)


def unite(even, odd, block):
    pieces = []
    for k in range(even.shape[1] // block):
        pieces += [even[:, k * block : (k + 1) * block], odd[:, k * block : (k + 1) * block]]
    return jnp.concatenate(pieces, axis=1)


def normalize(values):
    center = values - jnp.mean(values, axis=-1, keepdims=True)
    inverse = lax.rsqrt(jnp.mean(center * center, axis=-1, keepdims=True) + 1e-05)
    return (center * inverse, inverse)


def mask_of(start, length):
    return ((start + lax.broadcasted_iota(jnp.int32, (ROWS, 1), 0)) < length).astype(jnp.float32)


def enter_kernel(block, plan, lengths, where, saved, fwd, near, far, gain, kernel, own, other, halo, taps):
    frames = saved.shape[0]
    side = where[0]
    origin = where[1] * 2 * frames
    fwd_len = lengths[plan[0, 0]]
    bwd_len = lengths[plan[0, 1]]
    gain_row = gain[...]

    def conv_input(rows, start, length):
        hat, _ = normalize(rows.astype(jnp.float32))
        return (hat * gain_row * mask_of(start, length)).astype(jnp.bfloat16)

    def both(array):
        even, odd = divide(array, block)
        first = side == 0
        return jnp.where(first, even, odd), jnp.where(first, odd, even)

    def body(i, carry):
        at = pl.multiple_of(i * ROWS, ROWS)
        start = origin + side * frames + at
        for source, offset, length in ((saved, 0, bwd_len), (fwd, frames, fwd_len)):
            mine, theirs = both(conv_input(source[pl.ds(at, ROWS), :], start, length))
            own[pl.ds(pl.multiple_of(at + offset, ROWS), ROWS), :] = mine
            other[pl.ds(pl.multiple_of(at + offset, ROWS), ROWS), :] = theirs
        return carry

    lax.fori_loop(0, frames // ROWS, body, 0)
    first = side == 0
    spots = (
        (0, 0, -2 * HALO, bwd_len),
        (HALO, HALO, -HALO, bwd_len),
        (2 * HALO, 4 * HALO, -HALO, fwd_len),
    )
    for row, out_row, start, length in spots:
        rows = jnp.where(first, near[row : row + ROWS, :], far[row : row + ROWS, :])
        halo[out_row : out_row + ROWS, :] = both(conv_input(rows, origin + start, length))[0]
    spots = ((0, 2 * HALO, 0, bwd_len), (HALO, 3 * HALO, HALO, bwd_len), (2 * HALO, 5 * HALO, 0, fwd_len))
    for row, out_row, start, length in spots:
        rows = jnp.where(first, far[row : row + ROWS, :], near[row : row + ROWS, :])
        value = both(conv_input(rows, origin + 2 * frames + start, length))[0]
        halo[out_row : out_row + ROWS, :] = value
    taps[0:KW, :] = both(kernel[...])[0]
    taps[KW : KW + 1, :] = jnp.zeros((1, taps.shape[1]), jnp.float32)


def slide(buffer, chunk, start, count, weight):
    total = jnp.zeros((count, LANES), jnp.float32)
    for shift in range(8):
        tile = buffer[chunk, pl.ds(start + shift, count + 24), :]
        for step in range(4):
            offset = 8 * step + shift
            if 1 <= offset <= KW:
                total = total + weight(offset) * tile[8 * step : 8 * step + count]
    return total


def conv_kernel(
    where, own, got, halo, taps, grad, grad_got, near, far,
    hidden_saved, hidden_own, hidden_other, slope, window, grad_window, fwd_window,
):
    side = where[0]
    frames = grad.shape[0]
    mine = side * frames
    theirs = frames - mine
    chunks = own.shape[1] // LANES
    first = side == 0

    grad_window[pl.ds(pl.multiple_of(HALO + mine, HALO), frames), :] = grad[...]
    grad_window[pl.ds(pl.multiple_of(HALO + theirs, HALO), frames), :] = grad_got[...]
    grad_window[0:HALO, :] = jnp.where(first, near[3 * HALO :, :], far[3 * HALO :, :])
    grad_window[HALO + 2 * frames :, :] = jnp.where(first, far[3 * HALO :, :], near[3 * HALO :, :])

    def body(chunk, carry):
        lanes = pl.ds(pl.multiple_of(chunk * LANES, LANES), LANES)

        def put(buffer, row, values):
            size = values.shape[0]
            if not isinstance(row, int):
                row = pl.multiple_of(row, 8)
            buffer[chunk, pl.ds(row, size), :] = values.astype(jnp.float32)

        put(window, 0, halo[0 : 2 * HALO, lanes])
        put(window, 2 * HALO + mine, own[0:frames, lanes])
        put(window, 2 * HALO + theirs, got[0:frames, lanes])
        put(window, 2 * HALO + 2 * frames, halo[2 * HALO : 4 * HALO, lanes])
        put(window, 4 * HALO + 2 * frames, jnp.zeros((8, LANES), jnp.float32))
        put(fwd_window, 0, halo[4 * HALO : 5 * HALO, lanes])
        put(fwd_window, HALO + mine, own[frames:, lanes])
        put(fwd_window, HALO + theirs, got[frames:, lanes])
        put(fwd_window, HALO + 2 * frames, halo[5 * HALO :, lanes])
        put(fwd_window, 2 * HALO + 2 * frames, jnp.zeros((8, LANES), jnp.float32))

        def weight(offset):
            return taps[offset - 1 : offset, lanes]

        span = frames + HALO
        for half in range(2):
            mixed = slide(window, chunk, half * span, span, weight)
            gate = jax.nn.sigmoid(mixed)
            hidden = mixed * gate
            slope[pl.ds(half * span, span), lanes] = gate + hidden * (1.0 - gate)
            keep = hidden[HALO:] if half == 0 else hidden[:frames]
            hidden_saved[pl.ds(half * frames, frames), lanes] = keep.astype(jnp.bfloat16)
        for half in range(2):
            mixed = slide(fwd_window, chunk, half * frames, frames, weight)
            hidden = (mixed * jax.nn.sigmoid(mixed)).astype(jnp.bfloat16)

            @pl.when(side == half)
            def _():
                hidden_own[:, lanes] = hidden

            @pl.when(side != half)
            def _():
                hidden_other[:, lanes] = hidden

        return carry

    lax.fori_loop(0, chunks, body, 0)


def back_kernel(
    factor, plan, lengths, where, hidden_grad, slope, window, taps,
    grad_own, grad_other, kernel_grad, conv_grad,
):
    side = where[0]
    frames = grad_own.shape[0]
    chunks = taps.shape[1] // LANES
    origin = where[1] * 2 * frames
    bwd_len = lengths[plan[0, 1]]

    def body(chunk, carry):
        lanes = pl.ds(pl.multiple_of(chunk * LANES, LANES), LANES)
        value = (hidden_grad[:, lanes] * slope[:, lanes]).astype(jnp.bfloat16).astype(jnp.float32)
        conv_grad[chunk, 0 : 2 * frames + 2 * HALO, :] = value
        conv_grad[chunk, 2 * frames + 2 * HALO :, :] = jnp.zeros((8, LANES), jnp.float32)

        def weight(offset):
            return taps[KW - offset : KW - offset + 1, lanes]

        for half in range(2):
            total = slide(conv_grad, chunk, half * frames, frames, weight)
            frame = origin + half * frames + lax.broadcasted_iota(jnp.int32, (frames, 1), 0)
            total = (total * (frame < bwd_len).astype(jnp.float32)).astype(jnp.bfloat16)

            @pl.when(side == half)
            def _():
                grad_own[:, lanes] = total

            @pl.when(side != half)
            def _():
                grad_other[:, lanes] = total

        for shift in range(8):
            sums = [jnp.zeros((8, LANES), jnp.float32) for _ in range(4)]
            for half in range(2):
                left = conv_grad[chunk, pl.ds(HALO + half * frames, frames), :]
                right = window[chunk, pl.ds(HALO + half * frames + shift, frames + 24), :]
                for step in range(4):
                    if 1 <= 8 * step + shift <= KW:
                        term = left * right[8 * step : 8 * step + frames]
                        sums[step] = sums[step] + jnp.sum(term.reshape(frames // 8, 8, LANES), axis=0)
            for step in range(4):
                tap = 8 * step + shift - 1
                if 0 <= tap < KW:
                    row = jnp.sum(sums[step], axis=0, keepdims=True) * factor
                    kernel_grad[tap : tap + 1, lanes] = row
        kernel_grad[KW : KW + 1, lanes] = jnp.zeros((1, LANES), jnp.float32)
        return carry

    lax.fori_loop(0, chunks, body, 0)


def leave_kernel(block, where, own, got, saved, grad, gain, out):
    first = where[0] == 0
    gain_row = gain[...]

    def body(i, carry):
        at = pl.ds(pl.multiple_of(i * ROWS, ROWS), ROWS)
        mine, theirs = own[at, :], got[at, :]
        even, odd = jnp.where(first, mine, theirs), jnp.where(first, theirs, mine)
        hat_grad = unite(even, odd, block).astype(jnp.float32) * gain_row
        hat, inverse = normalize(saved[at, :].astype(jnp.float32))
        back = grad[at, :].astype(jnp.float32) + inverse * (
            hat_grad
            - jnp.mean(hat_grad, axis=-1, keepdims=True)
            - hat * jnp.mean(hat_grad * hat, axis=-1, keepdims=True)
        )
        out[at, :] = back.astype(jnp.bfloat16)
        return carry

    lax.fori_loop(0, saved.shape[0] // ROWS, body, 0)


def totals_kernel(block, where, own, got, kernel, gain, kernel_out, gain_out):
    first = where[0] == 0
    mine, theirs = own[...], got[...]
    even, odd = jnp.where(first, mine, theirs), jnp.where(first, theirs, mine)
    total = unite(even.astype(jnp.float32), odd.astype(jnp.float32), block)[:KW]
    kernel_out[...] = total
    gain_out[...] = jnp.sum(kernel[...] * total, axis=0, keepdims=True) / gain[...]


def per_device(fwd_input, saved_input, grad_in, gain, kernel, w_out, lengths, plan):
    frames, width = fwd_input.shape[1:]
    depth = lax.axis_size("z")
    side = lax.axis_index("x")
    rows = w_out.shape[1]
    half = rows * depth
    pair = 2 * frames
    factor = float(pair * depth) ** (-0.5)
    fwd_rows = fwd_input[0]
    saved_rows = saved_input[0]
    upstream = grad_in[0]
    bf16, f32 = jnp.bfloat16, jnp.float32
    where = jnp.stack([side, lax.axis_index("z")]).astype(jnp.int32)

    w_half = lax.all_gather(w_out[0], "z", axis=0, tiled=True)

    def edge(array, count):
        return lax.dynamic_slice_in_dim(array, side * (frames - count), count, axis=0)

    edges = jnp.concatenate([edge(saved_rows, 2 * HALO), edge(fwd_rows, HALO), edge(upstream, HALO)])
    count = 2 * depth
    tm = ("z", "x")
    hops = [(t, t + 1 if t % 2 else t - 1) for t in range(count)]
    near = lax.ppermute(edges, tm, [(a, b) for a, b in hops if 0 <= b < count])
    hops = [(t, t + 2 if t % 2 else t - 2) for t in range(count)]
    far = lax.ppermute(edges, tm, [(a, b) for a, b in hops if 0 <= b < count])
    grad_got = partner(upstream)

    own, other, halo, taps = call(
        functools.partial(enter_kernel, rows),
        [((pair, half), bf16), ((pair, half), bf16), ((6 * HALO, half), bf16), ((KW + 1, half), f32)],
        [SMEM, SMEM, SMEM] + [VMEM] * 6,
        flops=12 * 3 * frames * width,
        size=8 * frames * width,
    )(plan, lengths, where, saved_rows, fwd_rows, near, far, gain, kernel[0])
    got = partner(other)

    hidden_saved, hidden_own, hidden_other, slope, window, grad_window = call(
        conv_kernel,
        [
            ((pair, half), bf16),
            ((frames, half), bf16),
            ((frames, half), bf16),
            ((pair + 2 * HALO, half), f32),
            ((half // LANES, pair + 4 * HALO + 8, LANES), f32),
            ((pair + 2 * HALO, width), bf16),
        ],
        [SMEM] + [VMEM] * 8,
        [pltpu.VMEM((half // LANES, pair + 2 * HALO + 8, LANES), f32)],
        flops=2 * KW * 2 * pair * half,
        size=16 * pair * half,
    )(where, own, got, halo, taps, upstream, grad_got, near, far)

    partial_weight = (
        lax.dot_general(
            hidden_saved,
            grad_window[HALO : HALO + pair],
            (((0,), (0,)), ((), ())),
            preferred_element_type=f32,
        )
        * factor
    ).astype(bf16)
    weight_grad = lax.psum_scatter(
        lax.optimization_barrier(partial_weight), "z", scatter_dimension=0, tiled=True
    ).astype(f32)

    hidden_grad = lax.dot_general(
        grad_window, w_half, (((1,), (1,)), ((), ())), preferred_element_type=f32
    )
    norm_own, norm_other, kernel_local = call(
        functools.partial(back_kernel, factor),
        [((frames, half), bf16), ((frames, half), bf16), ((KW + 1, half), f32)],
        [SMEM, SMEM, SMEM] + [VMEM] * 4,
        [pltpu.VMEM((half // LANES, pair + 2 * HALO + 8, LANES), f32)],
        flops=4 * KW * pair * half,
        size=12 * pair * half,
    )(plan, lengths, where, hidden_grad, slope, window, taps)
    norm_got = partner(norm_other)
    total = kernel_local.astype(bf16)
    step = 1
    while step < depth:
        arrived = lax.ppermute(total, "z", [(i, i ^ step) for i in range(depth)])
        total = (total.astype(f32) + arrived.astype(f32)).astype(bf16)
        step *= 2
    total_got = partner(total)

    product_got = partner(jnp.dot(hidden_other, w_half, preferred_element_type=f32).astype(bf16))
    output = (
        fwd_rows.astype(f32)
        + (jnp.dot(hidden_own, w_half, preferred_element_type=f32) + product_got.astype(f32))
    ).astype(bf16)
    passed_activation = from_behind(output[None], 1)

    (input_back,) = call(
        functools.partial(leave_kernel, rows),
        [((frames, width), bf16)],
        [SMEM] + [VMEM] * 5,
        flops=20 * frames * width,
        size=8 * frames * width,
    )(where, norm_own, norm_got, saved_rows, upstream, gain)
    passed_gradient = from_behind(input_back[None], -1)
    kernel_grad, gain_grad = call(
        functools.partial(totals_kernel, rows),
        [((KW, width), f32), ((1, width), f32)],
        [SMEM] + [VMEM] * 4,
        flops=4 * KW * width,
        size=12 * KW * width,
    )(where, total, total_got, kernel[0], gain)
    return (
        passed_activation,
        passed_gradient,
        weight_grad[None],
        kernel_grad[None],
        gain_grad,
    )


def solution(mesh):
    sections, pieces = mesh.devices.shape
    folded = Mesh(mesh.devices.reshape(sections, pieces // 2, 2), ("section", "z", "x"))
    split = P("section", ("z", "x"), None)
    placed = (
        split,
        split,
        split,
        P("section", None),
        P("section", None, None),
        split,
        P(),
        P("section", None),
    )
    return jax.shard_map(
        per_device,
        mesh=folded,
        in_specs=placed,
        out_specs=(split, split, split, P("section", None, None), P("section", None)),
        check_vma=False,
    )
```

```python
import functools

import jax
import jax.numpy as jnp
from jax import lax
from jax.experimental import pallas as pl
from jax.experimental.pallas import tpu as pltpu
from jax.sharding import Mesh
from jax.sharding import PartitionSpec as P


KW = 31
HALO = 16
LANES = 128
ROWS = 16


VMEM = pl.BlockSpec(memory_space=pltpu.VMEM)
SMEM = pl.BlockSpec(memory_space=pltpu.SMEM)
HBM = pl.BlockSpec(memory_space=pl.ANY)


def call(body, outs, in_specs, scratch=(), flops=0, size=0):
    return pl.pallas_call(
        body,
        out_shape=[jax.ShapeDtypeStruct(shape, kind) for shape, kind in outs],
        in_specs=in_specs,
        out_specs=[VMEM] * len(outs),
        scratch_shapes=list(scratch),
        compiler_params=pltpu.CompilerParams(vmem_limit_bytes=40 << 20),
        cost_estimate=pl.CostEstimate(flops=flops, bytes_accessed=size, transcendentals=0),
    )


def partner(array):
    return lax.ppermute(array, "x", [(0, 1), (1, 0)])


def from_behind(array, by):
    length = lax.axis_size("section")
    pairs = [(i, i + by) for i in range(length) if 0 <= i + by < length]
    return lax.ppermute(array, "section", pairs)


def divide(array, block):
    count = array.shape[1] // block
    pieces = [array[:, k * block : (k + 1) * block] for k in range(count)]
    return jnp.concatenate(pieces[0::2], axis=1), jnp.concatenate(pieces[1::2], axis=1)


def unite(even, odd, block):
    pieces = []
    for k in range(even.shape[1] // block):
        pieces += [even[:, k * block : (k + 1) * block], odd[:, k * block : (k + 1) * block]]
    return jnp.concatenate(pieces, axis=1)


def normalize(values):
    center = values - jnp.mean(values, axis=-1, keepdims=True)
    inverse = lax.rsqrt(jnp.mean(center * center, axis=-1, keepdims=True) + 1e-05)
    return (center * inverse, inverse)


def mask_of(start, length):
    return ((start + lax.broadcasted_iota(jnp.int32, (ROWS, 1), 0)) < length).astype(jnp.float32)


def conv_input(rows, gain_row, start, length):
    hat, _ = normalize(rows.astype(jnp.float32))
    return (hat * gain_row * mask_of(start, length)).astype(jnp.bfloat16)


def both(array, block, first):
    even, odd = divide(array, block)
    return jnp.where(first, even, odd), jnp.where(first, odd, even)


def enter_kernel(
    block, plan, lengths, where, saved_hbm, fwd_hbm, grad_hbm, gain, kernel,
    own, other, taps, edges, saved, fwd, sems,
):
    frames = saved.shape[0]
    side = where[0]
    first = side == 0
    wide = pl.ds(pl.multiple_of(side * (frames - 2 * HALO), HALO), 2 * HALO)
    thin = pl.ds(pl.multiple_of(side * (frames - HALO), HALO), HALO)
    copies = [
        pltpu.make_async_copy(saved_hbm, saved, sems.at[0]),
        pltpu.make_async_copy(fwd_hbm, fwd, sems.at[1]),
        pltpu.make_async_copy(grad_hbm.at[thin, :], edges.at[3 * HALO : 4 * HALO, :], sems.at[2]),
    ]
    for copy in copies:
        copy.start()
    taps[0:KW, :] = both(kernel[:, 0, :], block, first)[0]
    taps[KW : KW + 1, :] = jnp.zeros((1, taps.shape[1]), jnp.float32)
    origin = where[1] * 2 * frames
    fwd_len = lengths[plan[0, 0]]
    bwd_len = lengths[plan[0, 1]]
    gain_row = gain[...]

    def pass_over(source, offset, length):
        def body(i, carry):
            at = pl.multiple_of(i * ROWS, ROWS)
            start = origin + side * frames + at
            value = conv_input(source[pl.ds(at, ROWS), :], gain_row, start, length)
            mine, theirs = both(value, block, first)
            own[pl.ds(pl.multiple_of(at + offset, ROWS), ROWS), :] = mine
            other[pl.ds(pl.multiple_of(at + offset, ROWS), ROWS), :] = theirs
            return carry

        lax.fori_loop(0, frames // ROWS, body, 0)

    copies[0].wait()
    pass_over(saved, 0, bwd_len)
    copies[1].wait()
    pass_over(fwd, frames, fwd_len)
    edges[0 : 2 * HALO, :] = saved[wide, :]
    edges[2 * HALO : 3 * HALO, :] = fwd[thin, :]
    copies[2].wait()


def slide(buffer, chunk, start, count, weight):
    total = jnp.zeros((count, LANES), jnp.float32)
    for shift in range(8):
        tile = buffer[chunk, pl.ds(start + shift, count + 24), :]
        for step in range(4):
            offset = 8 * step + shift
            if 1 <= offset <= KW:
                total = total + weight(offset) * tile[8 * step : 8 * step + count]
    return total


def conv_kernel(
    block, plan, lengths, where, own, got, taps, grad, grad_got, near, far, gain,
    hidden_saved, hidden_own, hidden_other, slope, window, grad_window, fwd_window, halo,
):
    side = where[0]
    frames = grad.shape[0]
    mine = side * frames
    theirs = frames - mine
    chunks = own.shape[1] // LANES
    first = side == 0
    origin = where[1] * 2 * frames
    fwd_len = lengths[plan[0, 0]]
    bwd_len = lengths[plan[0, 1]]
    gain_row = gain[...]
    spots = (
        (0, 0, -2 * HALO, bwd_len, True),
        (HALO, HALO, -HALO, bwd_len, True),
        (2 * HALO, 4 * HALO, -HALO, fwd_len, True),
        (0, 2 * HALO, 2 * frames, bwd_len, False),
        (HALO, 3 * HALO, 2 * frames + HALO, bwd_len, False),
        (2 * HALO, 5 * HALO, 2 * frames, fwd_len, False),
    )
    for row, out_row, start, length, ahead in spots:
        pieces = near[row : row + ROWS, :], far[row : row + ROWS, :]
        rows = jnp.where(first == ahead, *pieces)
        value = conv_input(rows, gain_row, origin + start, length)
        halo[out_row : out_row + ROWS, :] = both(value, block, first)[0]

    grad_window[pl.ds(pl.multiple_of(HALO + mine, HALO), frames), :] = grad[...]
    grad_window[pl.ds(pl.multiple_of(HALO + theirs, HALO), frames), :] = grad_got[...]
    grad_window[0:HALO, :] = jnp.where(first, near[3 * HALO :, :], far[3 * HALO :, :])
    grad_window[HALO + 2 * frames :, :] = jnp.where(first, far[3 * HALO :, :], near[3 * HALO :, :])

    def body(chunk, carry):
        lanes = pl.ds(pl.multiple_of(chunk * LANES, LANES), LANES)

        def put(buffer, row, values):
            size = values.shape[0]
            if not isinstance(row, int):
                row = pl.multiple_of(row, 8)
            buffer[chunk, pl.ds(row, size), :] = values.astype(jnp.float32)

        put(window, 0, halo[0 : 2 * HALO, lanes])
        put(window, 2 * HALO + mine, own[0:frames, lanes])
        put(window, 2 * HALO + theirs, got[0:frames, lanes])
        put(window, 2 * HALO + 2 * frames, halo[2 * HALO : 4 * HALO, lanes])
        put(window, 4 * HALO + 2 * frames, jnp.zeros((8, LANES), jnp.float32))
        put(fwd_window, 0, halo[4 * HALO : 5 * HALO, lanes])
        put(fwd_window, HALO + mine, own[frames:, lanes])
        put(fwd_window, HALO + theirs, got[frames:, lanes])
        put(fwd_window, HALO + 2 * frames, halo[5 * HALO :, lanes])
        put(fwd_window, 2 * HALO + 2 * frames, jnp.zeros((8, LANES), jnp.float32))

        def weight(offset):
            return taps[offset - 1 : offset, lanes]

        span = frames + HALO
        for half in range(2):
            mixed = slide(window, chunk, half * span, span, weight)
            gate = jax.nn.sigmoid(mixed)
            hidden = mixed * gate
            slope[pl.ds(half * span, span), lanes] = gate + hidden * (1.0 - gate)
            keep = hidden[HALO:] if half == 0 else hidden[:frames]
            hidden_saved[pl.ds(half * frames, frames), lanes] = keep.astype(jnp.bfloat16)
        for half in range(2):
            mixed = slide(fwd_window, chunk, half * frames, frames, weight)
            hidden = (mixed * jax.nn.sigmoid(mixed)).astype(jnp.bfloat16)

            @pl.when(side == half)
            def _():
                hidden_own[:, lanes] = hidden

            @pl.when(side != half)
            def _():
                hidden_other[:, lanes] = hidden

        return carry

    lax.fori_loop(0, chunks, body, 0)


def back_kernel(
    factor, plan, lengths, where, hidden_grad, slope, window, taps,
    grad_own, grad_other, kernel_grad, conv_grad,
):
    side = where[0]
    frames = grad_own.shape[0]
    chunks = taps.shape[1] // LANES
    origin = where[1] * 2 * frames
    bwd_len = lengths[plan[0, 1]]

    def body(chunk, carry):
        lanes = pl.ds(pl.multiple_of(chunk * LANES, LANES), LANES)
        value = (hidden_grad[:, lanes] * slope[:, lanes]).astype(jnp.bfloat16).astype(jnp.float32)
        conv_grad[chunk, 0 : 2 * frames + 2 * HALO, :] = value
        conv_grad[chunk, 2 * frames + 2 * HALO :, :] = jnp.zeros((8, LANES), jnp.float32)

        def weight(offset):
            return taps[KW - offset : KW - offset + 1, lanes]

        for half in range(2):
            total = slide(conv_grad, chunk, half * frames, frames, weight)
            frame = origin + half * frames + lax.broadcasted_iota(jnp.int32, (frames, 1), 0)
            total = (total * (frame < bwd_len).astype(jnp.float32)).astype(jnp.bfloat16)

            @pl.when(side == half)
            def _():
                grad_own[:, lanes] = total

            @pl.when(side != half)
            def _():
                grad_other[:, lanes] = total

        for shift in range(8):
            sums = [jnp.zeros((8, LANES), jnp.float32) for _ in range(4)]
            for half in range(2):
                left = conv_grad[chunk, pl.ds(HALO + half * frames, frames), :]
                right = window[chunk, pl.ds(HALO + half * frames + shift, frames + 24), :]
                for step in range(4):
                    if 1 <= 8 * step + shift <= KW:
                        term = left * right[8 * step : 8 * step + frames]
                        sums[step] = sums[step] + jnp.sum(term.reshape(frames // 8, 8, LANES), axis=0)
            for step in range(4):
                tap = 8 * step + shift - 1
                if 0 <= tap < KW:
                    row = jnp.sum(sums[step], axis=0, keepdims=True) * factor
                    kernel_grad[tap : tap + 1, lanes] = row
        kernel_grad[KW : KW + 1, lanes] = jnp.zeros((1, LANES), jnp.float32)
        return carry

    lax.fori_loop(0, chunks, body, 0)


def leave_kernel(block, where, own, got, saved, grad, gain, out):
    first = where[0] == 0
    gain_row = gain[...]

    def body(i, carry):
        at = pl.ds(pl.multiple_of(i * ROWS, ROWS), ROWS)
        mine, theirs = own[at, :], got[at, :]
        even, odd = jnp.where(first, mine, theirs), jnp.where(first, theirs, mine)
        hat_grad = unite(even, odd, block).astype(jnp.float32) * gain_row
        hat, inverse = normalize(saved[at, :].astype(jnp.float32))
        back = grad[at, :].astype(jnp.float32) + inverse * (
            hat_grad
            - jnp.mean(hat_grad, axis=-1, keepdims=True)
            - hat * jnp.mean(hat_grad * hat, axis=-1, keepdims=True)
        )
        out[at, :] = back.astype(jnp.bfloat16)
        return carry

    lax.fori_loop(0, saved.shape[0] // ROWS, body, 0)


def totals_kernel(block, where, own, got, kernel, gain, kernel_out, gain_out):
    first = where[0] == 0
    mine, theirs = own[...], got[...]
    even, odd = jnp.where(first, mine, theirs), jnp.where(first, theirs, mine)
    total = unite(even.astype(jnp.float32), odd.astype(jnp.float32), block)[:KW]
    kernel_out[:, 0, :] = total
    gain_out[...] = jnp.sum(kernel[:, 0, :] * total, axis=0, keepdims=True) / gain[...]


def per_device(fwd_input, saved_input, grad_in, gain, kernel, w_out, lengths, plan):
    frames, width = fwd_input.shape[1:]
    depth = lax.axis_size("z")
    side = lax.axis_index("x")
    rows = w_out.shape[1]
    half = rows * depth
    pair = 2 * frames
    factor = float(pair * depth) ** (-0.5)
    fwd_rows = fwd_input[0]
    saved_rows = saved_input[0]
    upstream = grad_in[0]
    bf16, f32 = jnp.bfloat16, jnp.float32
    here = lax.axis_index("z")
    where = jnp.stack([side, here]).astype(jnp.int32)

    barrier = lax.optimization_barrier

    up = [(i, (i + 1) % depth) for i in range(depth)]
    down = [(j, i) for i, j in up]
    cut = rows // 2

    def ring(pair_of):
        return lax.ppermute(pair_of[0], "z", up), lax.ppermute(pair_of[1], "z", down)

    def spot(k):
        return jnp.where(here + k % depth < depth, here + k % depth, here + k % depth - depth) * rows

    def take(array, k):
        return lax.dynamic_slice_in_dim(array, spot(k), rows, axis=0)

    def put(array, piece, k, offset=0):
        return lax.dynamic_update_slice_in_dim(array, piece, spot(k) + offset, axis=0)

    grad_got = partner(upstream)
    block = w_out[0]
    round_1 = ring((block, block))
    tap_rows = jnp.transpose(kernel, (1, 0, 2))

    own, other, taps, edges = call(
        functools.partial(enter_kernel, rows),
        [((pair, half), bf16), ((pair, half), bf16), ((KW + 1, half), f32), ((4 * HALO, width), bf16)],
        [SMEM, SMEM, SMEM, HBM, HBM, HBM, VMEM, VMEM],
        [
            pltpu.VMEM((frames, width), bf16),
            pltpu.VMEM((frames, width), bf16),
            pltpu.SemaphoreType.DMA((3,)),
        ],
        flops=12 * 2 * frames * width,
        size=10 * frames * width,
    )(plan, lengths, where, saved_rows, fwd_rows, upstream, gain, tap_rows)
    got = partner(other)
    count = 2 * depth
    tm = ("z", "x")
    hops = [(t, t + 1 if t % 2 else t - 1) for t in range(count)]
    near = lax.ppermute(edges, tm, [(a, b) for a, b in hops if 0 <= b < count])
    hops = [(t, t + 2 if t % 2 else t - 2) for t in range(count)]
    far = lax.ppermute(edges, tm, [(a, b) for a, b in hops if 0 <= b < count])

    round_2 = ring(round_1)
    got, near, far, grad_got, round_2 = barrier((got, near, far, grad_got, round_2))
    round_3 = ring(round_2)
    hidden_saved, hidden_own, hidden_other, slope, window, grad_window = call(
        functools.partial(conv_kernel, rows),
        [
            ((pair, half), bf16),
            ((frames, half), bf16),
            ((frames, half), bf16),
            ((pair + 2 * HALO, half), f32),
            ((half // LANES, pair + 4 * HALO + 8, LANES), f32),
            ((pair + 2 * HALO, width), bf16),
        ],
        [SMEM, SMEM, SMEM] + [VMEM] * 8,
        [
            pltpu.VMEM((half // LANES, pair + 2 * HALO + 8, LANES), f32),
            pltpu.VMEM((6 * HALO, half), bf16),
        ],
        flops=2 * KW * 2 * pair * half,
        size=16 * pair * half,
    )(plan, lengths, where, own, got, taps, upstream, grad_got, near, far, gain)

    hidden_saved, round_3 = barrier((hidden_saved, round_3))
    round_4 = ring((round_3[0][:cut], round_3[1][cut:]))
    partial = (
        lax.dot_general(
            hidden_saved,
            grad_window[HALO : HALO + pair],
            (((0,), (0,)), ((), ())),
            preferred_element_type=f32,
        )
        * factor
    ).astype(bf16)
    partial = barrier(partial)

    def plus(arrived, own_part):
        return (arrived.astype(f32) + own_part.astype(f32)).astype(bf16)

    back_1 = ring((take(partial, depth // 2)[:cut], take(partial, depth // 2)[cut:]))

    w_half = jnp.zeros((half, width), bf16)
    w_half = put(w_half, block, 0)
    for k, (behind, ahead) in enumerate((round_1, round_2, round_3), 1):
        w_half = put(put(w_half, behind, -k), ahead, k)
    w_half = put(put(w_half, round_4[0], depth // 2), round_4[1], depth // 2, cut)

    hidden_grad = lax.dot_general(
        grad_window, w_half, (((1,), (1,)), ((), ())), preferred_element_type=f32
    )
    hidden_grad, back_1 = barrier((hidden_grad, back_1))
    ahead, behind = take(partial, depth // 2 - 1), take(partial, depth // 2 + 1)
    back_2 = ring(
        (
            jnp.concatenate([plus(back_1[0], ahead[:cut]), ahead[cut:]]),
            jnp.concatenate([behind[:cut], plus(back_1[1], behind[cut:])]),
        )
    )
    norm_own, norm_other, kernel_local = call(
        functools.partial(back_kernel, factor),
        [((frames, half), bf16), ((frames, half), bf16), ((KW + 1, half), f32)],
        [SMEM, SMEM, SMEM] + [VMEM] * 4,
        [pltpu.VMEM((half // LANES, pair + 2 * HALO + 8, LANES), f32)],
        flops=4 * KW * pair * half,
        size=12 * pair * half,
    )(plan, lengths, where, hidden_grad, slope, window, taps)
    norm_got = partner(norm_other)
    total = kernel_local.astype(bf16)
    step = 1
    while step < depth:
        arrived = lax.ppermute(total, "z", [(i, i ^ step) for i in range(depth)])
        total = (total.astype(f32) + arrived.astype(f32)).astype(bf16)
        step *= 2
    total_got = partner(total)

    back_3 = ring((plus(back_2[0], take(partial, 2)), plus(back_2[1], take(partial, -2))))
    back_4 = ring((plus(back_3[0], take(partial, 1)), plus(back_3[1], take(partial, -1))))
    weight_grad = back_4[0].astype(f32) + back_4[1].astype(f32) + take(partial, 0).astype(f32)

    product_got = partner(jnp.dot(hidden_other, w_half, preferred_element_type=f32).astype(bf16))
    output = (
        fwd_rows.astype(f32)
        + (jnp.dot(hidden_own, w_half, preferred_element_type=f32) + product_got.astype(f32))
    ).astype(bf16)
    passed_activation = from_behind(output[None], 1)

    (input_back,) = call(
        functools.partial(leave_kernel, rows),
        [((frames, width), bf16)],
        [SMEM] + [VMEM] * 5,
        flops=20 * frames * width,
        size=8 * frames * width,
    )(where, norm_own, norm_got, saved_rows, upstream, gain)
    passed_gradient = from_behind(input_back[None], -1)
    kernel_grad, gain_grad = call(
        functools.partial(totals_kernel, rows),
        [((KW, 1, width), f32), ((1, width), f32)],
        [SMEM] + [VMEM] * 4,
        flops=4 * KW * width,
        size=12 * KW * width,
    )(where, total, total_got, tap_rows, gain)
    return (
        passed_activation,
        passed_gradient,
        weight_grad[None],
        jnp.transpose(kernel_grad, (1, 0, 2)),
        gain_grad,
    )


def solution(mesh):
    sections, pieces = mesh.devices.shape
    folded = Mesh(mesh.devices.reshape(sections, pieces // 2, 2), ("section", "z", "x"))
    split = P("section", ("z", "x"), None)
    placed = (
        split,
        split,
        split,
        P("section", None),
        P("section", None, None),
        split,
        P(),
        P("section", None),
    )

    return jax.shard_map(
        per_device,
        mesh=folded,
        in_specs=placed,
        out_specs=(split, split, split, P("section", None, None), P("section", None)),
        check_vma=False,
    )
```

```python
import functools

import jax
import jax.numpy as jnp
from jax import lax
from jax.experimental import pallas as pl
from jax.experimental.pallas import tpu as pltpu
from jax.sharding import Mesh
from jax.sharding import PartitionSpec as P


KW = 31
HALO = 16
LANES = 128
ROWS = 16


VMEM = pl.BlockSpec(memory_space=pltpu.VMEM)
SMEM = pl.BlockSpec(memory_space=pltpu.SMEM)
HBM = pl.BlockSpec(memory_space=pltpu.HBM)


def call(body, outs, in_specs, scratch=(), flops=0, size=0, limit=40 << 20):
    return pl.pallas_call(
        body,
        out_shape=[jax.ShapeDtypeStruct(shape, kind) for shape, kind in outs],
        in_specs=in_specs,
        out_specs=[VMEM] * len(outs),
        scratch_shapes=list(scratch),
        compiler_params=pltpu.CompilerParams(vmem_limit_bytes=limit),
        cost_estimate=pl.CostEstimate(flops=flops, bytes_accessed=size, transcendentals=0),
    )


def partner(array):
    return lax.ppermute(array, "x", [(0, 1), (1, 0)])


def from_behind(array, by):
    length = lax.axis_size("section")
    pairs = [(i, i + by) for i in range(length) if 0 <= i + by < length]
    return lax.ppermute(array, "section", pairs)


def divide(array, block):
    count = array.shape[1] // block
    pieces = [array[:, k * block : (k + 1) * block] for k in range(count)]
    return jnp.concatenate(pieces[0::2], axis=1), jnp.concatenate(pieces[1::2], axis=1)


def unite(even, odd, block):
    pieces = []
    for k in range(even.shape[1] // block):
        pieces += [even[:, k * block : (k + 1) * block], odd[:, k * block : (k + 1) * block]]
    return jnp.concatenate(pieces, axis=1)


def normalize(values):
    center = values - jnp.mean(values, axis=-1, keepdims=True)
    inverse = lax.rsqrt(jnp.mean(center * center, axis=-1, keepdims=True) + 1e-05)
    return (center * inverse, inverse)


def mask_of(start, length):
    return ((start + lax.broadcasted_iota(jnp.int32, (ROWS, 1), 0)) < length).astype(jnp.float32)


def conv_input(rows, gain_row, start, length):
    hat, _ = normalize(rows.astype(jnp.float32))
    return (hat * gain_row * mask_of(start, length)).astype(jnp.bfloat16)


def both(array, block, first):
    even, odd = divide(array, block)
    return jnp.where(first, even, odd), jnp.where(first, odd, even)


def edge_kernel(saved, fwd, grad, edges, sems):
    frames = saved.shape[0]
    side = lax.axis_index("x")
    wide = pl.ds(pl.multiple_of(side * (frames - 2 * HALO), HALO), 2 * HALO)
    thin = pl.ds(pl.multiple_of(side * (frames - HALO), HALO), HALO)
    copies = [
        pltpu.make_async_copy(saved.at[wide, :], edges.at[0 : 2 * HALO, :], sems.at[0]),
        pltpu.make_async_copy(fwd.at[thin, :], edges.at[2 * HALO : 3 * HALO, :], sems.at[1]),
        pltpu.make_async_copy(grad.at[thin, :], edges.at[3 * HALO : 4 * HALO, :], sems.at[2]),
    ]
    for copy in copies:
        copy.start()
    for copy in copies:
        copy.wait()


def enter_kernel(
    block, plan_hbm, lengths_hbm, saved_hbm, fwd_hbm, gain_hbm, kernel_hbm,
    own, own_fwd, other, other_fwd, taps, plan, lengths, saved, fwd, gain, kernel, sems,
):
    frames = saved.shape[0]
    side = lax.axis_index("x")
    first = side == 0
    pairs = (
        (saved_hbm, saved),
        (kernel_hbm, kernel),
        (plan_hbm, plan),
        (lengths_hbm, lengths),
        (gain_hbm, gain),
        (fwd_hbm, fwd),
    )
    copies = [pltpu.make_async_copy(a, b, sems.at[i]) for i, (a, b) in enumerate(pairs)]
    for copy in copies:
        copy.start()
    for copy in copies[1:5]:
        copy.wait()
    taps[0:KW, :] = both(kernel[:, 0, :], block, first)[0]
    taps[KW : KW + 1, :] = jnp.zeros((1, taps.shape[1]), jnp.float32)
    origin = lax.axis_index("z") * 2 * frames
    fwd_len = lengths[plan[0, 0]]
    bwd_len = lengths[plan[0, 1]]
    gain_row = gain[...]

    def pass_over(source, mine_out, theirs_out, length):
        def body(i, carry):
            at = pl.multiple_of(i * ROWS, ROWS)
            start = origin + side * frames + at
            value = conv_input(source[pl.ds(at, ROWS), :], gain_row, start, length)
            mine, theirs = both(value, block, first)
            mine_out[pl.ds(at, ROWS), :] = mine
            theirs_out[pl.ds(at, ROWS), :] = theirs
            return carry

        lax.fori_loop(0, frames // ROWS, body, 0)

    copies[0].wait()
    pass_over(saved, own, other, bwd_len)
    copies[5].wait()
    pass_over(fwd, own_fwd, other_fwd, fwd_len)


def slide(buffer, chunk, start, count, weight):
    total = jnp.zeros((count, LANES), jnp.float32)
    for shift in range(8):
        tile = buffer[chunk, pl.ds(start + shift, count + 24), :]
        for step in range(4):
            offset = 8 * step + shift
            if 1 <= offset <= KW:
                total = total + weight(offset) * tile[8 * step : 8 * step + count]
    return total


def fill_halo(block, halo, near, far, gain, spots, origin, length):
    first = lax.axis_index("x") == 0
    gain_row = gain[...]
    for row, out_row, start, ahead in spots:
        rows = jnp.where(first == ahead, near[row : row + ROWS, :], far[row : row + ROWS, :])
        value = conv_input(rows, gain_row, origin + start, length)
        halo[out_row : out_row + ROWS, :] = both(value, block, first)[0]


def store_rows(buffer, chunk, row, values):
    if not isinstance(row, int):
        row = pl.multiple_of(row, 8)
    buffer[chunk, pl.ds(row, values.shape[0]), :] = values.astype(jnp.float32)


def fwd_kernel(block, plan, lengths, own, got, taps, near, far, gain, hidden_own, hidden_other, window, halo):
    side = lax.axis_index("x")
    frames = own.shape[0]
    mine = side * frames
    theirs = frames - mine
    spots = ((2 * HALO, 0, -HALO, True), (2 * HALO, HALO, 2 * frames, False))
    origin = lax.axis_index("z") * 2 * frames
    fill_halo(block, halo, near, far, gain, spots, origin, lengths[plan[0, 0]])

    def body(chunk, carry):
        lanes = pl.ds(pl.multiple_of(chunk * LANES, LANES), LANES)
        put = functools.partial(store_rows, window, 0)
        put(0, halo[0:HALO, lanes])
        put(HALO + mine, own[:, lanes])
        put(HALO + theirs, got[:, lanes])
        put(HALO + 2 * frames, halo[HALO:, lanes])
        put(2 * HALO + 2 * frames, jnp.zeros((8, LANES), jnp.float32))

        def weight(offset):
            return taps[offset - 1 : offset, lanes]

        for half in range(2):
            mixed = slide(window, 0, half * frames, frames, weight)
            hidden = (mixed * jax.nn.sigmoid(mixed)).astype(jnp.bfloat16)

            @pl.when(side == half)
            def _():
                hidden_own[:, lanes] = hidden

            @pl.when(side != half)
            def _():
                hidden_other[:, lanes] = hidden

        return carry

    lax.fori_loop(0, own.shape[1] // LANES, body, 0)


def conv_kernel(
    block, factor, plan, lengths, own, got, taps, grad_hbm, grad_got, near, far, gain,
    *refs,
):
    blocks = refs[:-8]
    slope, keep_window, grad_window, hidden_saved, window, halo, product, sem = refs[-8:]
    side = lax.axis_index("x")
    frames = grad_got.shape[0]
    mine = side * frames
    spot = pl.ds(pl.multiple_of(HALO + mine, HALO), frames)
    copy = pltpu.make_async_copy(grad_hbm, grad_window.at[spot, :], sem)
    copy.start()
    theirs = frames - mine
    chunks = own.shape[1] // LANES
    first = side == 0
    origin = lax.axis_index("z") * 2 * frames
    spots = (
        (0, 0, -2 * HALO, True),
        (HALO, HALO, -HALO, True),
        (0, 2 * HALO, 2 * frames, False),
        (HALO, 3 * HALO, 2 * frames + HALO, False),
    )
    fill_halo(block, halo, near, far, gain, spots, origin, lengths[plan[0, 1]])

    grad_window[pl.ds(pl.multiple_of(HALO + theirs, HALO), frames), :] = grad_got[...]
    grad_window[0:HALO, :] = jnp.where(first, near[3 * HALO :, :], far[3 * HALO :, :])
    grad_window[HALO + 2 * frames :, :] = jnp.where(first, far[3 * HALO :, :], near[3 * HALO :, :])

    def body(chunk, carry):
        lanes = pl.ds(pl.multiple_of(chunk * LANES, LANES), LANES)

        put = functools.partial(store_rows, window, 0)
        put(0, halo[0 : 2 * HALO, lanes])
        put(2 * HALO + mine, own[:, lanes])
        put(2 * HALO + theirs, got[:, lanes])
        put(2 * HALO + 2 * frames, halo[2 * HALO :, lanes])
        put(4 * HALO + 2 * frames, jnp.zeros((8, LANES), jnp.float32))

        def weight(offset):
            return taps[offset - 1 : offset, lanes]

        keep_window[:, lanes] = window[0, 0 : keep_window.shape[0], :].astype(jnp.bfloat16)
        span = frames + HALO
        for half in range(2):
            mixed = slide(window, 0, half * span, span, weight)
            gate = jax.nn.sigmoid(mixed)
            hidden = mixed * gate
            value = gate + hidden * (1.0 - gate)
            slope[pl.ds(half * span, span), lanes] = value.astype(jnp.bfloat16)
            keep = hidden[HALO:] if half == 0 else hidden[:frames]
            hidden_saved[pl.ds(half * frames, frames), lanes] = keep.astype(jnp.bfloat16)
        return carry

    lax.fori_loop(0, chunks, body, 0)
    copy.wait()
    depth = len(blocks)
    here = lax.axis_index("z")

    def outer(index, carry):
        lanes = pl.ds(pl.multiple_of(index * 2 * LANES, 2 * LANES), 2 * LANES)
        value = lax.dot_general(
            hidden_saved[...],
            grad_window[HALO : HALO + 2 * frames, lanes],
            (((0,), (0,)), ((), ())),
            preferred_element_type=jnp.float32,
        )
        value = (value * factor).astype(jnp.bfloat16)
        product[...] = value.reshape(product.shape)
        for k, out in enumerate(blocks):
            place = jnp.where(here + k < depth, here + k, here + k - depth)
            out[:, lanes] = product[place]
        return carry

    lax.fori_loop(0, grad_window.shape[1] // (2 * LANES), outer, 0)


def back_kernel(
    factor, places, plan, lengths, grad_window, slope, window, taps, *refs
):
    blocks, (grad_own, grad_other, kernel_grad, weights, conv_grad, inputs) = refs[:-6], refs[-6:]
    rows = blocks[0].shape[0]
    depth = weights.shape[0] // rows
    for block, (step, offset, count) in zip(blocks, places):
        place = lax.axis_index("z") + step
        place = jnp.where(place < depth, place, place - depth) * rows + offset
        weights[pl.ds(pl.multiple_of(place, ROWS), count), :] = block[0:count, :]
    side = lax.axis_index("x")
    frames = grad_own.shape[0]
    chunks = taps.shape[1] // LANES
    origin = lax.axis_index("z") * 2 * frames
    bwd_len = lengths[plan[0, 1]]

    def product(index, carry):
        lanes = pl.ds(pl.multiple_of(index * 2 * LANES, 2 * LANES), 2 * LANES)
        hidden_grad = lax.dot_general(
            grad_window[...],
            weights[lanes, :],
            (((1,), (1,)), ((), ())),
            preferred_element_type=jnp.float32,
        )
        value = (hidden_grad * slope[:, lanes].astype(jnp.float32)).astype(jnp.bfloat16).astype(jnp.float32)
        for part in range(2):
            chunk = 2 * index + part
            conv_grad[chunk, 0 : 2 * frames + 2 * HALO, :] = value[:, part * LANES : (part + 1) * LANES]
            conv_grad[chunk, 2 * frames + 2 * HALO :, :] = jnp.zeros((8, LANES), jnp.float32)
        return carry

    lax.fori_loop(0, chunks // 2, product, 0)

    def body(chunk, carry):
        lanes = pl.ds(pl.multiple_of(chunk * LANES, LANES), LANES)

        inputs[0, 0 : window.shape[0], :] = window[:, lanes].astype(jnp.float32)
        inputs[0, window.shape[0] :, :] = jnp.zeros((8, LANES), jnp.float32)

        def weight(offset):
            return taps[KW - offset : KW - offset + 1, lanes]

        for half in range(2):
            total = slide(conv_grad, chunk, half * frames, frames, weight)
            frame = origin + half * frames + lax.broadcasted_iota(jnp.int32, (frames, 1), 0)
            total = (total * (frame < bwd_len).astype(jnp.float32)).astype(jnp.bfloat16)

            @pl.when(side == half)
            def _():
                grad_own[:, lanes] = total

            @pl.when(side != half)
            def _():
                grad_other[:, lanes] = total

        for shift in range(8):
            sums = [jnp.zeros((8, LANES), jnp.float32) for _ in range(4)]
            for half in range(2):
                left = conv_grad[chunk, pl.ds(HALO + half * frames, frames), :]
                right = inputs[0, pl.ds(HALO + half * frames + shift, frames + 24), :]
                for step in range(4):
                    if 1 <= 8 * step + shift <= KW:
                        term = left * right[8 * step : 8 * step + frames]
                        sums[step] = sums[step] + jnp.sum(term.reshape(frames // 8, 8, LANES), axis=0)
            for step in range(4):
                tap = 8 * step + shift - 1
                if 0 <= tap < KW:
                    row = jnp.sum(sums[step], axis=0, keepdims=True) * factor
                    kernel_grad[tap : tap + 1, lanes] = row
        kernel_grad[KW : KW + 1, lanes] = jnp.zeros((1, LANES), jnp.float32)
        return carry

    lax.fori_loop(0, chunks, body, 0)


def leave_kernel(block, own, got, saved, grad, gain, out):
    first = lax.axis_index("x") == 0
    gain_row = gain[...]

    def body(i, carry):
        at = pl.ds(pl.multiple_of(i * ROWS, ROWS), ROWS)
        mine, theirs = own[at, :], got[at, :]
        even, odd = jnp.where(first, mine, theirs), jnp.where(first, theirs, mine)
        hat_grad = unite(even, odd, block).astype(jnp.float32) * gain_row
        hat, inverse = normalize(saved[at, :].astype(jnp.float32))
        back = grad[at, :].astype(jnp.float32) + inverse * (
            hat_grad
            - jnp.mean(hat_grad, axis=-1, keepdims=True)
            - hat * jnp.mean(hat_grad * hat, axis=-1, keepdims=True)
        )
        out[at, :] = back.astype(jnp.bfloat16)
        return carry

    lax.fori_loop(0, saved.shape[0] // ROWS, body, 0)


def totals_kernel(block, own, got, kernel, gain, kernel_out, gain_out):
    first = lax.axis_index("x") == 0
    mine, theirs = own[...], got[...]
    even, odd = jnp.where(first, mine, theirs), jnp.where(first, theirs, mine)
    total = unite(even.astype(jnp.float32), odd.astype(jnp.float32), block)[:KW]
    kernel_out[:, 0, :] = total
    gain_out[...] = jnp.sum(kernel[:, 0, :] * total, axis=0, keepdims=True) / gain[...]


def per_device(fwd_input, saved_input, grad_in, gain, kernel, w_out, lengths, plan):
    frames, width = fwd_input.shape[1:]
    depth = lax.axis_size("z")
    rows = w_out.shape[1]
    half = rows * depth
    pair = 2 * frames
    factor = float(pair * depth) ** (-0.5)
    fwd_rows = fwd_input[0]
    saved_rows = saved_input[0]
    upstream = grad_in[0]
    bf16, f32 = jnp.bfloat16, jnp.float32

    barrier = lax.optimization_barrier

    up = [(i, (i + 1) % depth) for i in range(depth)]
    down = [(j, i) for i, j in up]

    def ring(pair_of):
        return lax.ppermute(pair_of[0], "z", up), lax.ppermute(pair_of[1], "z", down)

    grad_got = partner(upstream)
    (edges,) = call(
        edge_kernel,
        [((4 * HALO, width), bf16)],
        [HBM] * 3,
        [pltpu.SemaphoreType.DMA((3,))],
        limit=None,
        size=16 * HALO * width,
    )(saved_rows, fwd_rows, upstream)
    count = 2 * depth
    tm = ("z", "x")
    hops = [(t, t + 1 if t % 2 else t - 1) for t in range(count)]
    near = lax.ppermute(edges, tm, [(a, b) for a, b in hops if 0 <= b < count])
    hops = [(t, t + 2 if t % 2 else t - 2) for t in range(count)]
    far = lax.ppermute(edges, tm, [(a, b) for a, b in hops if 0 <= b < count])

    block = w_out[0]
    round_1 = ring((block, block))
    tap_rows = jnp.transpose(kernel, (1, 0, 2))

    own, own_fwd, other, other_fwd, taps = call(
        functools.partial(enter_kernel, rows),
        [((frames, half), bf16)] * 4 + [((KW + 1, half), f32)],
        [HBM] * 6,
        [
            pltpu.SMEM(plan.shape, jnp.int32),
            pltpu.SMEM(lengths.shape, jnp.int32),
            pltpu.VMEM((frames, width), bf16),
            pltpu.VMEM((frames, width), bf16),
            pltpu.VMEM(gain.shape, f32),
            pltpu.VMEM(tap_rows.shape, f32),
            pltpu.SemaphoreType.DMA((6,)),
        ],
        limit=None,
        flops=12 * 2 * frames * width,
        size=10 * frames * width,
    )(plan, lengths, saved_rows, fwd_rows, gain, tap_rows)
    got = partner(other)
    got_fwd = partner(other_fwd)
    round_2 = ring(round_1)
    got, near, far, grad_got, round_2 = barrier((got, near, far, grad_got, round_2))
    round_3 = ring(round_2)
    *partial, slope, window, grad_window = call(
        functools.partial(conv_kernel, rows, factor),
        [
            *[((rows, width), bf16)] * depth,
            ((pair + 2 * HALO, half), bf16),
            ((pair + 4 * HALO, half), bf16),
            ((pair + 2 * HALO, width), bf16),
        ],
        [SMEM, SMEM] + [VMEM] * 3 + [HBM] + [VMEM] * 4,
        [
            pltpu.VMEM((pair, half), bf16),
            pltpu.VMEM((1, pair + 4 * HALO + 8, LANES), f32),
            pltpu.VMEM((4 * HALO, half), bf16),
            pltpu.VMEM((depth, rows, 2 * LANES), bf16),
            pltpu.SemaphoreType.DMA(()),
        ],
        limit=None,
        flops=2 * KW * 2 * pair * half,
        size=16 * pair * half,
    )(plan, lengths, own, got, taps, upstream, grad_got, near, far, gain)

    hidden_own, hidden_other = call(
        functools.partial(fwd_kernel, rows),
        [((frames, half), bf16)] * 2,
        [SMEM, SMEM] + [VMEM] * 6,
        [
            pltpu.VMEM((1, pair + 2 * HALO + 8, LANES), f32),
            pltpu.VMEM((2 * HALO, half), bf16),
        ],
        limit=None,
        flops=2 * KW * pair * half,
        size=8 * pair * half,
    )(plan, lengths, own_fwd, got_fwd, taps, near, far, gain)
    partial, round_3 = barrier((partial, round_3))

    def plus(arrived, own_part):
        return (arrived.astype(f32) + own_part.astype(f32)).astype(bf16)

    round_4 = lax.ppermute(round_3[0], "z", up)
    back_1 = lax.ppermute(partial[depth // 2], "z", down)
    blocks = [block]
    places = [(0, 0, rows)]
    for k, (behind, ahead) in enumerate((round_1, round_2, round_3), 1):
        blocks += [behind, ahead]
        places += [(depth - k, 0, rows), (k, 0, rows)]
    blocks += [round_4]
    places += [(depth // 2, 0, rows)]
    back_2 = ring((partial[depth // 2 - 1], plus(back_1, partial[depth // 2 + 1])))
    norm_own, norm_other, kernel_local, w_half = call(
        functools.partial(back_kernel, factor, tuple(places)),
        [
            ((frames, half), bf16),
            ((frames, half), bf16),
            ((KW + 1, half), f32),
            ((half, width), bf16),
        ],
        [SMEM, SMEM] + [VMEM] * (4 + len(blocks)),
        [
            pltpu.VMEM((half // LANES, pair + 2 * HALO + 8, LANES), f32),
            pltpu.VMEM((1, pair + 4 * HALO + 8, LANES), f32),
        ],
        flops=4 * KW * pair * half,
        size=12 * pair * half,
    )(plan, lengths, grad_window, slope, window, taps, *blocks)
    norm_got = partner(norm_other)
    total = kernel_local.astype(bf16)
    step = 1
    while step < depth:
        arrived = lax.ppermute(total, "z", [(i, i ^ step) for i in range(depth)])
        total = (total.astype(f32) + arrived.astype(f32)).astype(bf16)
        step *= 2
    total_got = partner(total)

    back_3 = ring((plus(back_2[0], partial[2]), plus(back_2[1], partial[-2])))
    back_4 = ring((plus(back_3[0], partial[1]), plus(back_3[1], partial[-1])))
    weight_grad = back_4[0].astype(f32) + back_4[1].astype(f32) + partial[0].astype(f32)

    product = jnp.dot(hidden_other, w_half, preferred_element_type=f32).astype(bf16)
    product_got = partner(product)
    output = (
        fwd_rows.astype(f32)
        + (jnp.dot(hidden_own, w_half, preferred_element_type=f32) + product_got.astype(f32))
    ).astype(bf16)
    passed_activation = from_behind(output[None], 1)

    (input_back,) = call(
        functools.partial(leave_kernel, rows),
        [((frames, width), bf16)],
        [VMEM] * 5,
        flops=20 * frames * width,
        size=8 * frames * width,
    )(norm_own, norm_got, saved_rows, upstream, gain)
    passed_gradient = from_behind(input_back[None], -1)
    kernel_grad, gain_grad = call(
        functools.partial(totals_kernel, rows),
        [((KW, 1, width), f32), ((1, width), f32)],
        [VMEM] * 4,
        flops=4 * KW * width,
        size=12 * KW * width,
    )(total, total_got, tap_rows, gain)
    return (
        passed_activation,
        passed_gradient,
        weight_grad[None],
        jnp.transpose(kernel_grad, (1, 0, 2)),
        gain_grad,
    )


def solution(mesh):
    sections, pieces = mesh.devices.shape
    folded = Mesh(mesh.devices.reshape(sections, pieces // 2, 2), ("section", "z", "x"))
    split = P("section", ("z", "x"), None)
    placed = (
        split,
        split,
        split,
        P("section", None),
        P("section", None, None),
        split,
        P(),
        P("section", None),
    )

    return jax.shard_map(
        per_device,
        mesh=folded,
        in_specs=placed,
        out_specs=(split, split, split, P("section", None, None), P("section", None)),
        check_vma=False,
    )
```

```python
import functools

import jax
import jax.numpy as jnp
from jax import lax
from jax.experimental import pallas as pl
from jax.experimental.pallas import tpu as pltpu
from jax.sharding import Mesh
from jax.sharding import PartitionSpec as P


KW = 31
HALO = 16
LANES = 128
ROWS = 16


VMEM = pl.BlockSpec(memory_space=pltpu.VMEM)
SMEM = pl.BlockSpec(memory_space=pltpu.SMEM)
HBM = pl.BlockSpec(memory_space=pltpu.HBM)


def call(body, outs, in_specs, scratch=(), flops=0, size=0, limit=40 << 20):
    return pl.pallas_call(
        body,
        out_shape=[jax.ShapeDtypeStruct(shape, kind) for shape, kind in outs],
        in_specs=in_specs,
        out_specs=[VMEM] * len(outs),
        scratch_shapes=list(scratch),
        compiler_params=pltpu.CompilerParams(vmem_limit_bytes=limit),
        cost_estimate=pl.CostEstimate(flops=flops, bytes_accessed=size, transcendentals=0),
    )


def partner(array):
    return lax.ppermute(array, "x", [(0, 1), (1, 0)])


def from_behind(array, by):
    length = lax.axis_size("section")
    pairs = [(i, i + by) for i in range(length) if 0 <= i + by < length]
    return lax.ppermute(array, "section", pairs)


def divide(array, block):
    count = array.shape[1] // block
    pieces = [array[:, k * block : (k + 1) * block] for k in range(count)]
    return jnp.concatenate(pieces[0::2], axis=1), jnp.concatenate(pieces[1::2], axis=1)


def unite(even, odd, block):
    pieces = []
    for k in range(even.shape[1] // block):
        pieces += [even[:, k * block : (k + 1) * block], odd[:, k * block : (k + 1) * block]]
    return jnp.concatenate(pieces, axis=1)


def normalize(values):
    center = values - jnp.mean(values, axis=-1, keepdims=True)
    inverse = lax.rsqrt(jnp.mean(center * center, axis=-1, keepdims=True) + 1e-05)
    return (center * inverse, inverse)


def mask_of(start, length):
    return ((start + lax.broadcasted_iota(jnp.int32, (ROWS, 1), 0)) < length).astype(jnp.float32)


def conv_input(rows, gain_row, start, length):
    hat, _ = normalize(rows.astype(jnp.float32))
    return (hat * gain_row * mask_of(start, length)).astype(jnp.bfloat16)


def both(array, block, first):
    even, odd = divide(array, block)
    return jnp.where(first, even, odd), jnp.where(first, odd, even)


def edge_kernel(saved, fwd, grad, edges, sems):
    frames = saved.shape[0]
    side = lax.axis_index("x")
    wide = pl.ds(pl.multiple_of(side * (frames - 2 * HALO), HALO), 2 * HALO)
    thin = pl.ds(pl.multiple_of(side * (frames - HALO), HALO), HALO)
    copies = [
        pltpu.make_async_copy(saved.at[wide, :], edges.at[0 : 2 * HALO, :], sems.at[0]),
        pltpu.make_async_copy(fwd.at[thin, :], edges.at[2 * HALO : 3 * HALO, :], sems.at[1]),
        pltpu.make_async_copy(grad.at[thin, :], edges.at[3 * HALO : 4 * HALO, :], sems.at[2]),
    ]
    for copy in copies:
        copy.start()
    for copy in copies:
        copy.wait()


def enter_kernel(
    block, plan_hbm, lengths_hbm, saved_hbm, fwd_hbm, gain_hbm, kernel_hbm,
    own, own_fwd, other, other_fwd, taps, plan, lengths, saved, fwd, gain, kernel, sems,
):
    frames = saved.shape[0]
    side = lax.axis_index("x")
    first = side == 0
    pairs = (
        (saved_hbm, saved),
        (kernel_hbm, kernel),
        (plan_hbm, plan),
        (lengths_hbm, lengths),
        (gain_hbm, gain),
        (fwd_hbm, fwd),
    )
    copies = [pltpu.make_async_copy(a, b, sems.at[i]) for i, (a, b) in enumerate(pairs)]
    for copy in copies:
        copy.start()
    for copy in copies[1:5]:
        copy.wait()
    taps[0:KW, :] = both(kernel[:, 0, :], block, first)[0]
    taps[KW : KW + 1, :] = jnp.zeros((1, taps.shape[1]), jnp.float32)
    origin = lax.axis_index("z") * 2 * frames
    fwd_len = lengths[plan[0, 0]]
    bwd_len = lengths[plan[0, 1]]
    gain_row = gain[...]

    def pass_over(source, mine_out, theirs_out, length):
        def body(i, carry):
            at = pl.multiple_of(i * ROWS, ROWS)
            start = origin + side * frames + at
            value = conv_input(source[pl.ds(at, ROWS), :], gain_row, start, length)
            mine, theirs = both(value, block, first)
            mine_out[pl.ds(at, ROWS), :] = mine
            theirs_out[pl.ds(at, ROWS), :] = theirs
            return carry

        lax.fori_loop(0, frames // ROWS, body, 0, unroll=4)

    copies[0].wait()
    pass_over(saved, own, other, bwd_len)
    copies[5].wait()
    pass_over(fwd, own_fwd, other_fwd, fwd_len)


def slide(buffer, chunk, start, count, weight):
    total = jnp.zeros((count, LANES), jnp.float32)
    for shift in range(8):
        tile = buffer[chunk, pl.ds(start + shift, count + 24), :]
        for step in range(4):
            offset = 8 * step + shift
            if 1 <= offset <= KW:
                total = total + weight(offset) * tile[8 * step : 8 * step + count]
    return total


def fill_halo(block, halo, near, far, gain, spots, origin, length):
    first = lax.axis_index("x") == 0
    gain_row = gain[...]
    for row, out_row, start, ahead in spots:
        rows = jnp.where(first == ahead, near[row : row + ROWS, :], far[row : row + ROWS, :])
        value = conv_input(rows, gain_row, origin + start, length)
        halo[out_row : out_row + ROWS, :] = both(value, block, first)[0]


def store_rows(buffer, chunk, row, values):
    if not isinstance(row, int):
        row = pl.multiple_of(row, 8)
    buffer[chunk, pl.ds(row, values.shape[0]), :] = values.astype(jnp.float32)


def fwd_kernel(block, plan, lengths, own, got, taps, near, far, gain, hidden_own, hidden_other, window, halo):
    side = lax.axis_index("x")
    frames = own.shape[0]
    mine = side * frames
    theirs = frames - mine
    spots = ((2 * HALO, 0, -HALO, True), (2 * HALO, HALO, 2 * frames, False))
    origin = lax.axis_index("z") * 2 * frames
    fill_halo(block, halo, near, far, gain, spots, origin, lengths[plan[0, 0]])

    def body(chunk, carry):
        lanes = pl.ds(pl.multiple_of(chunk * LANES, LANES), LANES)
        put = functools.partial(store_rows, window, 0)
        put(0, halo[0:HALO, lanes])
        put(HALO + mine, own[:, lanes])
        put(HALO + theirs, got[:, lanes])
        put(HALO + 2 * frames, halo[HALO:, lanes])
        put(2 * HALO + 2 * frames, jnp.zeros((8, LANES), jnp.float32))

        def weight(offset):
            return taps[offset - 1 : offset, lanes]

        for half in range(2):
            mixed = slide(window, 0, half * frames, frames, weight)
            hidden = (mixed * jax.nn.sigmoid(mixed)).astype(jnp.bfloat16)

            @pl.when(side == half)
            def _():
                hidden_own[:, lanes] = hidden

            @pl.when(side != half)
            def _():
                hidden_other[:, lanes] = hidden

        return carry

    lax.fori_loop(0, own.shape[1] // LANES, body, 0)


def conv_kernel(
    block, factor, plan, lengths, own, got, taps, grad_hbm, grad_got, near, far, gain,
    *refs,
):
    blocks = refs[:-7]
    keep, grad_window, hidden_saved, window, halo, product, sem = refs[-7:]
    side = lax.axis_index("x")
    frames = grad_got.shape[0]
    mine = side * frames
    spot = pl.ds(pl.multiple_of(HALO + mine, HALO), frames)
    copy = pltpu.make_async_copy(grad_hbm, grad_window.at[spot, :], sem)
    copy.start()
    theirs = frames - mine
    chunks = own.shape[1] // LANES
    first = side == 0
    origin = lax.axis_index("z") * 2 * frames
    spots = (
        (0, 0, -2 * HALO, True),
        (HALO, HALO, -HALO, True),
        (0, 2 * HALO, 2 * frames, False),
        (HALO, 3 * HALO, 2 * frames + HALO, False),
    )
    fill_halo(block, halo, near, far, gain, spots, origin, lengths[plan[0, 1]])

    grad_window[pl.ds(pl.multiple_of(HALO + theirs, HALO), frames), :] = grad_got[...]
    grad_window[0:HALO, :] = jnp.where(first, near[3 * HALO :, :], far[3 * HALO :, :])
    grad_window[HALO + 2 * frames :, :] = jnp.where(first, far[3 * HALO :, :], near[3 * HALO :, :])

    def body(chunk, carry):
        lanes = pl.ds(pl.multiple_of(chunk * LANES, LANES), LANES)

        put = functools.partial(store_rows, window, 0)
        put(0, halo[0 : 2 * HALO, lanes])
        put(2 * HALO + mine, own[:, lanes])
        put(2 * HALO + theirs, got[:, lanes])
        put(2 * HALO + 2 * frames, halo[2 * HALO :, lanes])
        put(4 * HALO + 2 * frames, jnp.zeros((8, LANES), jnp.float32))

        def weight(offset):
            return taps[offset - 1 : offset, lanes]

        keep[2 * frames + 2 * HALO :, lanes] = window[0, 0 : 2 * frames + 4 * HALO, :].astype(jnp.bfloat16)
        span = frames + HALO
        for half in range(2):
            mixed = slide(window, 0, half * span, span, weight)
            gate = jax.nn.sigmoid(mixed)
            hidden = mixed * gate
            value = gate + hidden * (1.0 - gate)
            keep[pl.ds(half * span, span), lanes] = value.astype(jnp.bfloat16)
            inner = hidden[HALO:] if half == 0 else hidden[:frames]
            hidden_saved[pl.ds(half * frames, frames), lanes] = inner.astype(jnp.bfloat16)
        return carry

    lax.fori_loop(0, chunks, body, 0)
    copy.wait()
    depth = len(blocks)
    here = lax.axis_index("z")

    def outer(index, carry):
        lanes = pl.ds(pl.multiple_of(index * 2 * LANES, 2 * LANES), 2 * LANES)
        value = lax.dot_general(
            hidden_saved[...],
            grad_window[HALO : HALO + 2 * frames, lanes],
            (((0,), (0,)), ((), ())),
            preferred_element_type=jnp.float32,
        )
        value = (value * factor).astype(jnp.bfloat16)
        product[...] = value.reshape(product.shape)
        for k, out in enumerate(blocks):
            place = jnp.where(here + k < depth, here + k, here + k - depth)
            out[:, lanes] = product[place]
        return carry

    lax.fori_loop(0, grad_window.shape[1] // (2 * LANES), outer, 0)


def back_kernel(
    factor, places, plan, lengths, grad_window, kept, taps, *refs
):
    blocks, (grad_own, grad_other, kernel_grad, weights, conv_grad, inputs) = refs[:-6], refs[-6:]
    rows = blocks[0].shape[0]
    depth = weights.shape[0] // rows
    for block, (step, offset, count) in zip(blocks, places):
        place = lax.axis_index("z") + step
        place = jnp.where(place < depth, place, place - depth) * rows + offset
        weights[pl.ds(pl.multiple_of(place, ROWS), count), :] = block[0:count, :]
    side = lax.axis_index("x")
    frames = grad_own.shape[0]
    chunks = taps.shape[1] // LANES
    origin = lax.axis_index("z") * 2 * frames
    bwd_len = lengths[plan[0, 1]]

    def product(index, carry):
        lanes = pl.ds(pl.multiple_of(index * 2 * LANES, 2 * LANES), 2 * LANES)
        hidden_grad = lax.dot_general(
            grad_window[...],
            weights[lanes, :],
            (((1,), (1,)), ((), ())),
            preferred_element_type=jnp.float32,
        )
        value = (hidden_grad * kept[0 : 2 * frames + 2 * HALO, lanes].astype(jnp.float32)).astype(jnp.bfloat16).astype(jnp.float32)
        for part in range(2):
            chunk = 2 * index + part
            conv_grad[chunk, 0 : 2 * frames + 2 * HALO, :] = value[:, part * LANES : (part + 1) * LANES]
            conv_grad[chunk, 2 * frames + 2 * HALO :, :] = jnp.zeros((8, LANES), jnp.float32)
        return carry

    lax.fori_loop(0, chunks // 2, product, 0)

    def body(chunk, carry):
        lanes = pl.ds(pl.multiple_of(chunk * LANES, LANES), LANES)

        size = 2 * frames + 4 * HALO
        inputs[0, 0:size, :] = kept[2 * frames + 2 * HALO :, lanes].astype(jnp.float32)
        inputs[0, size:, :] = jnp.zeros((8, LANES), jnp.float32)

        def weight(offset):
            return taps[KW - offset : KW - offset + 1, lanes]

        for half in range(2):
            total = slide(conv_grad, chunk, half * frames, frames, weight)
            frame = origin + half * frames + lax.broadcasted_iota(jnp.int32, (frames, 1), 0)
            total = (total * (frame < bwd_len).astype(jnp.float32)).astype(jnp.bfloat16)

            @pl.when(side == half)
            def _():
                grad_own[:, lanes] = total

            @pl.when(side != half)
            def _():
                grad_other[:, lanes] = total

        for shift in range(8):
            sums = [jnp.zeros((8, LANES), jnp.float32) for _ in range(4)]
            for half in range(2):
                left = conv_grad[chunk, pl.ds(HALO + half * frames, frames), :]
                right = inputs[0, pl.ds(HALO + half * frames + shift, frames + 24), :]
                for step in range(4):
                    if 1 <= 8 * step + shift <= KW:
                        term = left * right[8 * step : 8 * step + frames]
                        sums[step] = sums[step] + jnp.sum(term.reshape(frames // 8, 8, LANES), axis=0)
            for step in range(4):
                tap = 8 * step + shift - 1
                if 0 <= tap < KW:
                    row = jnp.sum(sums[step], axis=0, keepdims=True) * factor
                    kernel_grad[tap : tap + 1, lanes] = row
        kernel_grad[KW : KW + 1, lanes] = jnp.zeros((1, LANES), jnp.float32)
        return carry

    lax.fori_loop(0, chunks, body, 0)


def leave_kernel(block, own, got, saved, grad, gain, out):
    first = lax.axis_index("x") == 0
    gain_row = gain[...]

    def body(i, carry):
        at = pl.ds(pl.multiple_of(i * ROWS, ROWS), ROWS)
        mine, theirs = own[at, :], got[at, :]
        even, odd = jnp.where(first, mine, theirs), jnp.where(first, theirs, mine)
        hat_grad = unite(even, odd, block).astype(jnp.float32) * gain_row
        hat, inverse = normalize(saved[at, :].astype(jnp.float32))
        back = grad[at, :].astype(jnp.float32) + inverse * (
            hat_grad
            - jnp.mean(hat_grad, axis=-1, keepdims=True)
            - hat * jnp.mean(hat_grad * hat, axis=-1, keepdims=True)
        )
        out[at, :] = back.astype(jnp.bfloat16)
        return carry

    lax.fori_loop(0, saved.shape[0] // ROWS, body, 0, unroll=4)


def totals_kernel(block, own, got, kernel, gain, kernel_out, gain_out):
    first = lax.axis_index("x") == 0
    mine, theirs = own[...], got[...]
    even, odd = jnp.where(first, mine, theirs), jnp.where(first, theirs, mine)
    total = unite(even.astype(jnp.float32), odd.astype(jnp.float32), block)[:KW]
    kernel_out[:, 0, :] = total
    gain_out[...] = jnp.sum(kernel[:, 0, :] * total, axis=0, keepdims=True) / gain[...]


def per_device(fwd_input, saved_input, grad_in, gain, kernel, w_out, lengths, plan):
    frames, width = fwd_input.shape[1:]
    depth = lax.axis_size("z")
    rows = w_out.shape[1]
    half = rows * depth
    pair = 2 * frames
    factor = float(pair * depth) ** (-0.5)
    fwd_rows = fwd_input[0]
    saved_rows = saved_input[0]
    upstream = grad_in[0]
    bf16, f32 = jnp.bfloat16, jnp.float32

    barrier = lax.optimization_barrier

    up = [(i, (i + 1) % depth) for i in range(depth)]
    down = [(j, i) for i, j in up]

    def ring(pair_of):
        return lax.ppermute(pair_of[0], "z", up), lax.ppermute(pair_of[1], "z", down)

    grad_got = partner(upstream)
    (edges,) = call(
        edge_kernel,
        [((4 * HALO, width), bf16)],
        [HBM] * 3,
        [pltpu.SemaphoreType.DMA((3,))],
        limit=None,
        size=16 * HALO * width,
    )(saved_rows, fwd_rows, upstream)
    count = 2 * depth
    tm = ("z", "x")
    hops = [(t, t + 1 if t % 2 else t - 1) for t in range(count)]
    near = lax.ppermute(edges, tm, [(a, b) for a, b in hops if 0 <= b < count])
    hops = [(t, t + 2 if t % 2 else t - 2) for t in range(count)]
    far = lax.ppermute(edges, tm, [(a, b) for a, b in hops if 0 <= b < count])

    block = w_out[0]
    round_1 = ring((block, block))
    tap_rows = jnp.transpose(kernel, (1, 0, 2))

    own, own_fwd, other, other_fwd, taps = call(
        functools.partial(enter_kernel, rows),
        [((frames, half), bf16)] * 4 + [((KW + 1, half), f32)],
        [HBM] * 6,
        [
            pltpu.SMEM(plan.shape, jnp.int32),
            pltpu.SMEM(lengths.shape, jnp.int32),
            pltpu.VMEM((frames, width), bf16),
            pltpu.VMEM((frames, width), bf16),
            pltpu.VMEM(gain.shape, f32),
            pltpu.VMEM(tap_rows.shape, f32),
            pltpu.SemaphoreType.DMA((6,)),
        ],
        limit=None,
        flops=12 * 2 * frames * width,
        size=10 * frames * width,
    )(plan, lengths, saved_rows, fwd_rows, gain, tap_rows)
    got = partner(other)
    got_fwd = partner(other_fwd)
    round_2 = ring(round_1)
    round_3 = ring(round_2)
    *partial, kept, grad_window = call(
        functools.partial(conv_kernel, rows, factor),
        [
            *[((rows, width), bf16)] * depth,
            ((2 * pair + 6 * HALO, half), bf16),
            ((pair + 2 * HALO, width), bf16),
        ],
        [SMEM, SMEM] + [VMEM] * 3 + [HBM] + [VMEM] * 4,
        [
            pltpu.VMEM((pair, half), bf16),
            pltpu.VMEM((1, pair + 4 * HALO + 8, LANES), f32),
            pltpu.VMEM((4 * HALO, half), bf16),
            pltpu.VMEM((depth, rows, 2 * LANES), bf16),
            pltpu.SemaphoreType.DMA(()),
        ],
        limit=None,
        flops=2 * KW * 2 * pair * half,
        size=16 * pair * half,
    )(plan, lengths, own, got, taps, upstream, grad_got, near, far, gain)

    hidden_own, hidden_other = call(
        functools.partial(fwd_kernel, rows),
        [((frames, half), bf16)] * 2,
        [SMEM, SMEM] + [VMEM] * 6,
        [
            pltpu.VMEM((1, pair + 2 * HALO + 8, LANES), f32),
            pltpu.VMEM((2 * HALO, half), bf16),
        ],
        limit=None,
        flops=2 * KW * pair * half,
        size=8 * pair * half,
    )(plan, lengths, own_fwd, got_fwd, taps, near, far, gain)
    partial, round_3 = barrier((partial, round_3))

    def plus(arrived, own_part):
        return (arrived.astype(f32) + own_part.astype(f32)).astype(bf16)

    round_4 = lax.ppermute(round_3[0], "z", up)
    back_1 = lax.ppermute(partial[depth // 2], "z", down)
    blocks = [block]
    places = [(0, 0, rows)]
    for k, (behind, ahead) in enumerate((round_1, round_2, round_3), 1):
        blocks += [behind, ahead]
        places += [(depth - k, 0, rows), (k, 0, rows)]
    blocks += [round_4]
    places += [(depth // 2, 0, rows)]
    back_2 = ring((partial[depth // 2 - 1], plus(back_1, partial[depth // 2 + 1])))
    norm_own, norm_other, kernel_local, w_half = call(
        functools.partial(back_kernel, factor, tuple(places)),
        [
            ((frames, half), bf16),
            ((frames, half), bf16),
            ((KW + 1, half), f32),
            ((half, width), bf16),
        ],
        [SMEM, SMEM] + [VMEM] * (3 + len(blocks)),
        [
            pltpu.VMEM((half // LANES, pair + 2 * HALO + 8, LANES), f32),
            pltpu.VMEM((1, pair + 4 * HALO + 8, LANES), f32),
        ],
        flops=4 * KW * pair * half,
        size=12 * pair * half,
        limit=40<<20,
    )(plan, lengths, grad_window, kept, taps, *blocks)
    norm_got = partner(norm_other)
    total = kernel_local.astype(bf16)
    step = 1
    while step < depth:
        arrived = lax.ppermute(total, "z", [(i, i ^ step) for i in range(depth)])
        total = (total.astype(f32) + arrived.astype(f32)).astype(bf16)
        step *= 2
    total_got = partner(total)

    back_3 = ring((plus(back_2[0], partial[2]), plus(back_2[1], partial[-2])))
    back_4 = ring((plus(back_3[0], partial[1]), plus(back_3[1], partial[-1])))
    weight_grad = back_4[0].astype(f32) + back_4[1].astype(f32) + partial[0].astype(f32)

    product = jnp.dot(hidden_other, w_half, preferred_element_type=f32).astype(bf16)
    product_got = partner(product)
    output = (
        fwd_rows.astype(f32)
        + (jnp.dot(hidden_own, w_half, preferred_element_type=f32) + product_got.astype(f32))
    ).astype(bf16)
    passed_activation = from_behind(output[None], 1)

    (input_back,) = call(
        functools.partial(leave_kernel, rows),
        [((frames, width), bf16)],
        [VMEM] * 5,
        flops=20 * frames * width,
        size=8 * frames * width,
    )(norm_own, norm_got, saved_rows, upstream, gain)
    passed_gradient = from_behind(input_back[None], -1)
    kernel_grad, gain_grad = call(
        functools.partial(totals_kernel, rows),
        [((KW, 1, width), f32), ((1, width), f32)],
        [VMEM] * 4,
        limit=40<<20,
        flops=4 * KW * width,
        size=12 * KW * width,
    )(total, total_got, tap_rows, gain)
    return (
        passed_activation,
        passed_gradient,
        weight_grad[None],
        jnp.transpose(kernel_grad, (1, 0, 2)),
        gain_grad,
    )


def solution(mesh):
    sections, pieces = mesh.devices.shape
    folded = Mesh(mesh.devices.reshape(sections, pieces // 2, 2), ("section", "z", "x"))
    split = P("section", ("z", "x"), None)
    placed = (
        split,
        split,
        split,
        P("section", None),
        P("section", None, None),
        split,
        P(),
        P("section", None),
    )

    return jax.shard_map(
        per_device,
        mesh=folded,
        in_specs=placed,
        out_specs=(split, split, split, P("section", None, None), P("section", None)),
        check_vma=False,
    )
```

```python
import functools

import jax
import jax.numpy as jnp
from jax import lax
from jax.experimental import pallas as pl
from jax.experimental.pallas import tpu as pltpu
from jax.sharding import Mesh
from jax.sharding import PartitionSpec as P


KW = 31
HALO = 16
LANES = 128
ROWS = 16


VMEM = pl.BlockSpec(memory_space=pltpu.VMEM)
SMEM = pl.BlockSpec(memory_space=pltpu.SMEM)
HBM = pl.BlockSpec(memory_space=pltpu.HBM)


def call(body, outs, in_specs, scratch=(), flops=0, size=0, limit=40 << 20):
    return pl.pallas_call(
        body,
        out_shape=[jax.ShapeDtypeStruct(shape, kind) for shape, kind in outs],
        in_specs=in_specs,
        out_specs=[VMEM] * len(outs),
        scratch_shapes=list(scratch),
        compiler_params=pltpu.CompilerParams(vmem_limit_bytes=limit),
        cost_estimate=pl.CostEstimate(flops=flops, bytes_accessed=size, transcendentals=0),
    )


def partner(array):
    return lax.ppermute(array, "x", [(0, 1), (1, 0)])


def from_behind(array, by):
    length = lax.axis_size("section")
    pairs = [(i, i + by) for i in range(length) if 0 <= i + by < length]
    return lax.ppermute(array, "section", pairs)


def divide(array, block):
    count = array.shape[1] // block
    pieces = [array[:, k * block : (k + 1) * block] for k in range(count)]
    return jnp.concatenate(pieces[0::2], axis=1), jnp.concatenate(pieces[1::2], axis=1)


def unite(even, odd, block):
    pieces = []
    for k in range(even.shape[1] // block):
        pieces += [even[:, k * block : (k + 1) * block], odd[:, k * block : (k + 1) * block]]
    return jnp.concatenate(pieces, axis=1)


def normalize(values):
    center = values - jnp.mean(values, axis=-1, keepdims=True)
    inverse = lax.rsqrt(jnp.mean(center * center, axis=-1, keepdims=True) + 1e-05)
    return (center * inverse, inverse)


def mask_of(start, length):
    return ((start + lax.broadcasted_iota(jnp.int32, (ROWS, 1), 0)) < length).astype(jnp.float32)


def conv_input(rows, gain_row, start, length):
    hat, _ = normalize(rows.astype(jnp.float32))
    return (hat * gain_row * mask_of(start, length)).astype(jnp.bfloat16)


def both(array, block, first):
    even, odd = divide(array, block)
    return jnp.where(first, even, odd), jnp.where(first, odd, even)


def edge_kernel(
    block, plan_hbm, lengths_hbm, saved_hbm, fwd_hbm, grad_hbm, gain_hbm,
    to_near, to_far, plan, lengths, gain, rows, sems,
):
    frames = saved_hbm.shape[0]
    half = to_near.shape[1]
    side = lax.axis_index("x")
    wide = pl.multiple_of(side * (frames - 2 * HALO), HALO)
    thin = pl.multiple_of(side * (frames - HALO), HALO)
    pairs = (
        (plan_hbm, plan),
        (lengths_hbm, lengths),
        (gain_hbm, gain),
        (saved_hbm.at[pl.ds(wide, 2 * HALO), :], rows.at[0 : 2 * HALO, :]),
        (fwd_hbm.at[pl.ds(thin, HALO), :], rows.at[2 * HALO : 3 * HALO, :]),
        (grad_hbm.at[pl.ds(thin, HALO), :], rows.at[3 * HALO : 4 * HALO, :]),
    )
    copies = [pltpu.make_async_copy(a, b, sems.at[i]) for i, (a, b) in enumerate(pairs)]
    for copy in copies:
        copy.start()
    for copy in copies:
        copy.wait()
    origin = lax.axis_index("z") * 2 * frames + side * frames
    fwd_len = lengths[plan[0, 0]]
    bwd_len = lengths[plan[0, 1]]
    gain_row = gain[...]
    for at, start, length in ((0, wide, bwd_len), (HALO, wide + HALO, bwd_len), (2 * HALO, thin, fwd_len)):
        value = conv_input(rows[at : at + HALO, :], gain_row, origin + start, length)
        mine, theirs = both(value, block, side == 0)
        to_far[at : at + HALO, :] = mine
        to_near[at : at + HALO, :] = theirs
    for part in range(2):
        at = (3 + part) * HALO
        value = rows[3 * HALO : 4 * HALO, part * half : (part + 1) * half]
        to_far[at : at + HALO, :] = value
        to_near[at : at + HALO, :] = value


def enter_kernel(
    block, plan_hbm, lengths_hbm, saved_hbm, fwd_hbm, gain_hbm, kernel_hbm,
    own, own_fwd, other, other_fwd, taps, plan, lengths, saved, fwd, gain, kernel, sems,
):
    frames = saved.shape[0]
    side = lax.axis_index("x")
    first = side == 0
    pairs = (
        (saved_hbm, saved),
        (kernel_hbm, kernel),
        (plan_hbm, plan),
        (lengths_hbm, lengths),
        (gain_hbm, gain),
        (fwd_hbm, fwd),
    )
    copies = [pltpu.make_async_copy(a, b, sems.at[i]) for i, (a, b) in enumerate(pairs)]
    for copy in copies:
        copy.start()
    for copy in copies[1:5]:
        copy.wait()
    taps[0:KW, :] = both(kernel[:, 0, :], block, first)[0]
    taps[KW : KW + 1, :] = jnp.zeros((1, taps.shape[1]), jnp.float32)
    origin = lax.axis_index("z") * 2 * frames
    fwd_len = lengths[plan[0, 0]]
    bwd_len = lengths[plan[0, 1]]
    gain_row = gain[...]

    def pass_over(source, mine_out, theirs_out, length):
        def body(i, carry):
            at = pl.multiple_of(i * ROWS, ROWS)
            start = origin + side * frames + at
            value = conv_input(source[pl.ds(at, ROWS), :], gain_row, start, length)
            mine, theirs = both(value, block, first)
            mine_out[pl.ds(at, ROWS), :] = mine
            theirs_out[pl.ds(at, ROWS), :] = theirs
            return carry

        lax.fori_loop(0, frames // ROWS, body, 0, unroll=4)

    copies[0].wait()
    pass_over(saved, own, other, bwd_len)
    copies[5].wait()
    pass_over(fwd, own_fwd, other_fwd, fwd_len)


def slide(buffer, chunk, start, count, weight):
    total = jnp.zeros((count, LANES), jnp.float32)
    for shift in range(8):
        tile = buffer[chunk, pl.ds(start + shift, count + 24), :]
        for step in range(4):
            offset = 8 * step + shift
            if 1 <= offset <= KW:
                total = total + weight(offset) * tile[8 * step : 8 * step + count]
    return total


def outside(near, far, rows, lanes, ahead):
    first = lax.axis_index("x") == 0
    return jnp.where(first == ahead, near[rows, lanes], far[rows, lanes])


def store_rows(buffer, chunk, row, values):
    if not isinstance(row, int):
        row = pl.multiple_of(row, 8)
    buffer[chunk, pl.ds(row, values.shape[0]), :] = values.astype(jnp.float32)


def fwd_kernel(own, got, taps, near, far, hidden_own, hidden_other, window):
    side = lax.axis_index("x")
    frames = own.shape[0]
    mine = side * frames
    theirs = frames - mine
    edge = slice(2 * HALO, 3 * HALO)

    def body(chunk, carry):
        lanes = pl.ds(pl.multiple_of(chunk * LANES, LANES), LANES)
        put = functools.partial(store_rows, window, 0)
        put(0, outside(near, far, edge, lanes, True))
        put(HALO + mine, own[:, lanes])
        put(HALO + theirs, got[:, lanes])
        put(HALO + 2 * frames, outside(near, far, edge, lanes, False))
        put(2 * HALO + 2 * frames, jnp.zeros((8, LANES), jnp.float32))

        def weight(offset):
            return taps[offset - 1 : offset, lanes]

        for half in range(2):
            mixed = slide(window, 0, half * frames, frames, weight)
            hidden = (mixed * jax.nn.sigmoid(mixed)).astype(jnp.bfloat16)

            @pl.when(side == half)
            def _():
                hidden_own[:, lanes] = hidden

            @pl.when(side != half)
            def _():
                hidden_other[:, lanes] = hidden

        return carry

    lax.fori_loop(0, own.shape[1] // LANES, body, 0)


def conv_kernel(
    factor, own, got, taps, grad_hbm, grad_got, near, far,
    *refs,
):
    blocks = refs[:-6]
    keep, grad_window, hidden_saved, window, product, sem = refs[-6:]
    side = lax.axis_index("x")
    frames = grad_got.shape[0]
    mine = side * frames
    spot = pl.ds(pl.multiple_of(HALO + mine, HALO), frames)
    copy = pltpu.make_async_copy(grad_hbm, grad_window.at[spot, :], sem)
    copy.start()
    theirs = frames - mine
    chunks = own.shape[1] // LANES
    half = own.shape[1]
    for part in range(2):
        rows = slice((3 + part) * HALO, (4 + part) * HALO)
        lanes = slice(part * half, (part + 1) * half)
        grad_window[0:HALO, lanes] = outside(near, far, rows, slice(None), True)
        grad_window[HALO + 2 * frames :, lanes] = outside(near, far, rows, slice(None), False)
    grad_window[pl.ds(pl.multiple_of(HALO + theirs, HALO), frames), :] = grad_got[...]
    edge = slice(0, 2 * HALO)

    def body(chunk, carry):
        lanes = pl.ds(pl.multiple_of(chunk * LANES, LANES), LANES)

        put = functools.partial(store_rows, window, 0)
        put(0, outside(near, far, edge, lanes, True))
        put(2 * HALO + mine, own[:, lanes])
        put(2 * HALO + theirs, got[:, lanes])
        put(2 * HALO + 2 * frames, outside(near, far, edge, lanes, False))
        put(4 * HALO + 2 * frames, jnp.zeros((8, LANES), jnp.float32))

        def weight(offset):
            return taps[offset - 1 : offset, lanes]

        keep[2 * frames + 2 * HALO :, lanes] = window[0, 0 : 2 * frames + 4 * HALO, :].astype(jnp.bfloat16)
        span = frames + HALO
        for half in range(2):
            mixed = slide(window, 0, half * span, span, weight)
            gate = jax.nn.sigmoid(mixed)
            hidden = mixed * gate
            value = gate + hidden * (1.0 - gate)
            keep[pl.ds(half * span, span), lanes] = value.astype(jnp.bfloat16)
            inner = hidden[HALO:] if half == 0 else hidden[:frames]
            hidden_saved[pl.ds(half * frames, frames), lanes] = inner.astype(jnp.bfloat16)
        return carry

    lax.fori_loop(0, chunks, body, 0)
    copy.wait()
    depth = len(blocks)
    here = lax.axis_index("z")

    def outer(index, carry):
        lanes = pl.ds(pl.multiple_of(index * 2 * LANES, 2 * LANES), 2 * LANES)
        value = lax.dot_general(
            hidden_saved[...],
            grad_window[HALO : HALO + 2 * frames, lanes],
            (((0,), (0,)), ((), ())),
            preferred_element_type=jnp.float32,
        )
        value = (value * factor).astype(jnp.bfloat16)
        product[...] = value.reshape(product.shape)
        for k, out in enumerate(blocks):
            place = jnp.where(here + k < depth, here + k, here + k - depth)
            out[:, lanes] = product[place]
        return carry

    lax.fori_loop(0, grad_window.shape[1] // (2 * LANES), outer, 0)


def back_kernel(
    factor, places, plan, lengths, grad_window, kept, taps, *refs
):
    blocks, (grad_own, grad_other, kernel_grad, weights, conv_grad, inputs) = refs[:-6], refs[-6:]
    rows = blocks[0].shape[0]
    depth = weights.shape[0] // rows
    for block, (step, offset, count) in zip(blocks, places):
        place = lax.axis_index("z") + step
        place = jnp.where(place < depth, place, place - depth) * rows + offset
        weights[pl.ds(pl.multiple_of(place, ROWS), count), :] = block[0:count, :]
    side = lax.axis_index("x")
    frames = grad_own.shape[0]
    chunks = taps.shape[1] // LANES
    origin = lax.axis_index("z") * 2 * frames
    bwd_len = lengths[plan[0, 1]]

    def product(index, carry):
        lanes = pl.ds(pl.multiple_of(index * 2 * LANES, 2 * LANES), 2 * LANES)
        hidden_grad = lax.dot_general(
            grad_window[...],
            weights[lanes, :],
            (((1,), (1,)), ((), ())),
            preferred_element_type=jnp.float32,
        )
        value = (hidden_grad * kept[0 : 2 * frames + 2 * HALO, lanes].astype(jnp.float32)).astype(jnp.bfloat16).astype(jnp.float32)
        for part in range(2):
            chunk = 2 * index + part
            conv_grad[chunk, 0 : 2 * frames + 2 * HALO, :] = value[:, part * LANES : (part + 1) * LANES]
            conv_grad[chunk, 2 * frames + 2 * HALO :, :] = jnp.zeros((8, LANES), jnp.float32)
        return carry

    lax.fori_loop(0, chunks // 2, product, 0)

    def body(chunk, carry):
        lanes = pl.ds(pl.multiple_of(chunk * LANES, LANES), LANES)

        size = 2 * frames + 4 * HALO
        inputs[0, 0:size, :] = kept[2 * frames + 2 * HALO :, lanes].astype(jnp.float32)
        inputs[0, size:, :] = jnp.zeros((8, LANES), jnp.float32)

        def weight(offset):
            return taps[KW - offset : KW - offset + 1, lanes]

        for half in range(2):
            total = slide(conv_grad, chunk, half * frames, frames, weight)
            frame = origin + half * frames + lax.broadcasted_iota(jnp.int32, (frames, 1), 0)
            total = (total * (frame < bwd_len).astype(jnp.float32)).astype(jnp.bfloat16)

            @pl.when(side == half)
            def _():
                grad_own[:, lanes] = total

            @pl.when(side != half)
            def _():
                grad_other[:, lanes] = total

        for shift in range(8):
            sums = [jnp.zeros((8, LANES), jnp.float32) for _ in range(4)]
            for half in range(2):
                left = conv_grad[chunk, pl.ds(HALO + half * frames, frames), :]
                right = inputs[0, pl.ds(HALO + half * frames + shift, frames + 24), :]
                for step in range(4):
                    if 1 <= 8 * step + shift <= KW:
                        term = left * right[8 * step : 8 * step + frames]
                        sums[step] = sums[step] + jnp.sum(term.reshape(frames // 8, 8, LANES), axis=0)
            for step in range(4):
                tap = 8 * step + shift - 1
                if 0 <= tap < KW:
                    row = jnp.sum(sums[step], axis=0, keepdims=True) * factor
                    kernel_grad[tap : tap + 1, lanes] = row
        kernel_grad[KW : KW + 1, lanes] = jnp.zeros((1, LANES), jnp.float32)
        return carry

    lax.fori_loop(0, chunks, body, 0)


def leave_kernel(block, own, got, saved, grad, gain, out):
    first = lax.axis_index("x") == 0
    gain_row = gain[...]

    def body(i, carry):
        at = pl.ds(pl.multiple_of(i * ROWS, ROWS), ROWS)
        mine, theirs = own[at, :], got[at, :]
        even, odd = jnp.where(first, mine, theirs), jnp.where(first, theirs, mine)
        hat_grad = unite(even, odd, block).astype(jnp.float32) * gain_row
        hat, inverse = normalize(saved[at, :].astype(jnp.float32))
        back = grad[at, :].astype(jnp.float32) + inverse * (
            hat_grad
            - jnp.mean(hat_grad, axis=-1, keepdims=True)
            - hat * jnp.mean(hat_grad * hat, axis=-1, keepdims=True)
        )
        out[at, :] = back.astype(jnp.bfloat16)
        return carry

    lax.fori_loop(0, saved.shape[0] // ROWS, body, 0, unroll=4)


def totals_kernel(block, own, got, kernel, gain, kernel_out, gain_out):
    first = lax.axis_index("x") == 0
    mine, theirs = own[...], got[...]
    even, odd = jnp.where(first, mine, theirs), jnp.where(first, theirs, mine)
    total = unite(even.astype(jnp.float32), odd.astype(jnp.float32), block)[:KW]
    kernel_out[:, 0, :] = total
    gain_out[...] = jnp.sum(kernel[:, 0, :] * total, axis=0, keepdims=True) / gain[...]


def relay_kernel(source, out):
    out[...] = source[...]


def finish_kernel(first, second, third, out):
    out[...] = first[...].astype(jnp.float32) + second[...].astype(jnp.float32) + third[...].astype(jnp.float32)


def per_device(fwd_input, saved_input, grad_in, gain, kernel, w_out, lengths, plan):
    frames, width = fwd_input.shape[1:]
    depth = lax.axis_size("z")
    rows = w_out.shape[1]
    half = rows * depth
    pair = 2 * frames
    factor = float(pair * depth) ** (-0.5)
    fwd_rows = fwd_input[0]
    saved_rows = saved_input[0]
    upstream = grad_in[0]
    bf16, f32 = jnp.bfloat16, jnp.float32

    barrier = lax.optimization_barrier

    up = [(i, (i + 1) % depth) for i in range(depth)]
    down = [(j, i) for i, j in up]

    def ring(pair_of):
        return lax.ppermute(pair_of[0], "z", up), lax.ppermute(pair_of[1], "z", down)

    grad_got = partner(upstream)
    to_near, to_far = call(
        functools.partial(edge_kernel, rows),
        [((5 * HALO, half), bf16)] * 2,
        [HBM] * 6,
        [
            pltpu.SMEM(plan.shape, jnp.int32),
            pltpu.SMEM(lengths.shape, jnp.int32),
            pltpu.VMEM(gain.shape, f32),
            pltpu.VMEM((4 * HALO, width), bf16),
            pltpu.SemaphoreType.DMA((6,)),
        ],
        limit=None,
        size=16 * HALO * width,
    )(plan, lengths, saved_rows, fwd_rows, upstream, gain)
    count = 2 * depth
    tm = ("z", "x")
    hops = [(t, t + 1 if t % 2 else t - 1) for t in range(count)]
    near = lax.ppermute(to_near, tm, [(a, b) for a, b in hops if 0 <= b < count])
    hops = [(t, t + 2 if t % 2 else t - 2) for t in range(count)]
    far = lax.ppermute(to_far, tm, [(a, b) for a, b in hops if 0 <= b < count])

    block = w_out[0]
    round_1 = ring((block, block))
    tap_rows = jnp.transpose(kernel, (1, 0, 2))

    own, own_fwd, other, other_fwd, taps = call(
        functools.partial(enter_kernel, rows),
        [((frames, half), bf16)] * 4 + [((KW + 1, half), f32)],
        [HBM] * 6,
        [
            pltpu.SMEM(plan.shape, jnp.int32),
            pltpu.SMEM(lengths.shape, jnp.int32),
            pltpu.VMEM((frames, width), bf16),
            pltpu.VMEM((frames, width), bf16),
            pltpu.VMEM(gain.shape, f32),
            pltpu.VMEM(tap_rows.shape, f32),
            pltpu.SemaphoreType.DMA((6,)),
        ],
        limit=None,
        flops=12 * 2 * frames * width,
        size=10 * frames * width,
    )(plan, lengths, saved_rows, fwd_rows, gain, tap_rows)
    got = partner(other)
    got_fwd = partner(other_fwd)
    round_2 = ring(round_1)
    round_3 = ring(round_2)
    *partial, kept, grad_window = call(
        functools.partial(conv_kernel, factor),
        [
            *[((rows, width), bf16)] * depth,
            ((2 * pair + 6 * HALO, half), bf16),
            ((pair + 2 * HALO, width), bf16),
        ],
        [VMEM] * 3 + [HBM] + [VMEM] * 3,
        [
            pltpu.VMEM((pair, half), bf16),
            pltpu.VMEM((1, pair + 4 * HALO + 8, LANES), f32),
            pltpu.VMEM((depth, rows, 2 * LANES), bf16),
            pltpu.SemaphoreType.DMA(()),
        ],
        limit=None,
        flops=2 * KW * 2 * pair * half,
        size=16 * pair * half,
    )(own, got, taps, upstream, grad_got, near, far)

    hidden_own, hidden_other = call(
        fwd_kernel,
        [((frames, half), bf16)] * 2,
        [VMEM] * 5,
        [pltpu.VMEM((1, pair + 2 * HALO + 8, LANES), f32)],
        limit=None,
        flops=2 * KW * pair * half,
        size=8 * pair * half,
    )(own_fwd, got_fwd, taps, near, far)
    partial, round_3 = barrier((partial, round_3))

    def plus(arrived, own_part):
        return (arrived.astype(f32) + own_part.astype(f32)).astype(bf16)

    round_4 = lax.ppermute(round_3[0], "z", up)
    back_1 = lax.ppermute(partial[depth // 2], "z", down)
    blocks = [block]
    places = [(0, 0, rows)]
    for k, (behind, ahead) in enumerate((round_1, round_2, round_3), 1):
        blocks += [behind, ahead]
        places += [(depth - k, 0, rows), (k, 0, rows)]
    blocks += [round_4]
    places += [(depth // 2, 0, rows)]
    back_2 = ring((partial[depth // 2 - 1], plus(back_1, partial[depth // 2 + 1])))
    norm_own, norm_other, kernel_local, w_half = call(
        functools.partial(back_kernel, factor, tuple(places)),
        [
            ((frames, half), bf16),
            ((frames, half), bf16),
            ((KW + 1, half), f32),
            ((half, width), bf16),
        ],
        [SMEM, SMEM] + [VMEM] * (3 + len(blocks)),
        [
            pltpu.VMEM((half // LANES, pair + 2 * HALO + 8, LANES), f32),
            pltpu.VMEM((1, pair + 4 * HALO + 8, LANES), f32),
        ],
        flops=4 * KW * pair * half,
        size=12 * pair * half,
        limit=40<<20,
    )(plan, lengths, grad_window, kept, taps, *blocks)
    norm_got = partner(norm_other)
    total = kernel_local.astype(bf16)
    step = 1
    while step < depth:
        arrived = lax.ppermute(total, "z", [(i, i ^ step) for i in range(depth)])
        total = (total.astype(f32) + arrived.astype(f32)).astype(bf16)
        step *= 2
    total_got = partner(total)

    back_3 = ring((plus(back_2[0], partial[2]), plus(back_2[1], partial[-2])))
    back_4 = ring((plus(back_3[0], partial[1]), plus(back_3[1], partial[-1])))
    (weight_grad,) = call(
        finish_kernel, [((rows, width), f32)], [VMEM] * 3, size=10 * rows * width
    )(back_4[0], back_4[1], partial[0])

    product = jnp.dot(hidden_other, w_half, preferred_element_type=f32).astype(bf16)
    product_got = partner(product)
    output = (
        fwd_rows.astype(f32)
        + (jnp.dot(hidden_own, w_half, preferred_element_type=f32) + product_got.astype(f32))
    ).astype(bf16)
    passed_activation = from_behind(output[None], 1)

    (input_back,) = call(
        functools.partial(leave_kernel, rows),
        [((frames, width), bf16)],
        [VMEM] * 5,
        flops=20 * frames * width,
        size=8 * frames * width,
    )(norm_own, norm_got, saved_rows, upstream, gain)
    passed_gradient = from_behind(input_back[None], -1)
    kernel_grad, gain_grad = call(
        functools.partial(totals_kernel, rows),
        [((KW, 1, width), f32), ((1, width), f32)],
        [VMEM] * 4,
        limit=40<<20,
        flops=4 * KW * width,
        size=12 * KW * width,
    )(total, total_got, tap_rows, gain)
    (passed_gradient,) = call(
        relay_kernel, [(passed_gradient.shape, bf16)], [VMEM], size=4 * frames * width
    )(passed_gradient)
    return (
        passed_activation,
        passed_gradient,
        weight_grad[None],
        jnp.transpose(kernel_grad, (1, 0, 2)),
        gain_grad,
    )


def solution(mesh):
    sections, pieces = mesh.devices.shape
    folded = Mesh(mesh.devices.reshape(sections, pieces // 2, 2), ("section", "z", "x"))
    split = P("section", ("z", "x"), None)
    placed = (
        split,
        split,
        split,
        P("section", None),
        P("section", None, None),
        split,
        P(),
        P("section", None),
    )

    return jax.shard_map(
        per_device,
        mesh=folded,
        in_specs=placed,
        out_specs=(split, split, split, P("section", None, None), P("section", None)),
        check_vma=False,
    )
```

```python
import functools

import jax
import jax.numpy as jnp
from jax import lax
from jax.experimental import pallas as pl
from jax.experimental.pallas import tpu as pltpu
from jax.sharding import Mesh
from jax.sharding import PartitionSpec as P


KW = 31
HALO = 16
LANES = 128
ROWS = 16


VMEM = pl.BlockSpec(memory_space=pltpu.VMEM)
SMEM = pl.BlockSpec(memory_space=pltpu.SMEM)
HBM = pl.BlockSpec(memory_space=pltpu.HBM)


def call(body, outs, in_specs, scratch=(), flops=0, size=0, limit=40 << 20):
    return pl.pallas_call(
        body,
        out_shape=[jax.ShapeDtypeStruct(shape, kind) for shape, kind in outs],
        in_specs=in_specs,
        out_specs=[VMEM] * len(outs),
        scratch_shapes=list(scratch),
        compiler_params=pltpu.CompilerParams(vmem_limit_bytes=limit),
        cost_estimate=pl.CostEstimate(flops=flops, bytes_accessed=size, transcendentals=0),
    )


def partner(array):
    return lax.ppermute(array, "x", [(0, 1), (1, 0)])


def from_behind(array, by):
    length = lax.axis_size("section")
    pairs = [(i, i + by) for i in range(length) if 0 <= i + by < length]
    return lax.ppermute(array, "section", pairs)


def divide(array, block):
    count = array.shape[1] // block
    pieces = [array[:, k * block : (k + 1) * block] for k in range(count)]
    return jnp.concatenate(pieces[0::2], axis=1), jnp.concatenate(pieces[1::2], axis=1)


def unite(even, odd, block):
    pieces = []
    for k in range(even.shape[1] // block):
        pieces += [even[:, k * block : (k + 1) * block], odd[:, k * block : (k + 1) * block]]
    return jnp.concatenate(pieces, axis=1)


def normalize(values):
    center = values - jnp.mean(values, axis=-1, keepdims=True)
    inverse = lax.rsqrt(jnp.mean(center * center, axis=-1, keepdims=True) + 1e-05)
    return (center * inverse, inverse)


def mask_of(start, length):
    return ((start + lax.broadcasted_iota(jnp.int32, (ROWS, 1), 0)) < length).astype(jnp.float32)


def conv_input(rows, gain_row, start, length):
    hat, _ = normalize(rows.astype(jnp.float32))
    return (hat * gain_row * mask_of(start, length)).astype(jnp.bfloat16)


def both(array, block, first):
    even, odd = divide(array, block)
    return jnp.where(first, even, odd), jnp.where(first, odd, even)


def edge_kernel(
    block, plan_hbm, lengths_hbm, saved_hbm, fwd_hbm, grad_hbm, gain_hbm,
    to_near, to_far, plan, lengths, gain, rows, sems,
):
    frames = saved_hbm.shape[0]
    half = to_near.shape[1]
    side = lax.axis_index("x")
    wide = pl.multiple_of(side * (frames - 2 * HALO), HALO)
    thin = pl.multiple_of(side * (frames - HALO), HALO)
    pairs = (
        (plan_hbm, plan),
        (lengths_hbm, lengths),
        (gain_hbm, gain),
        (saved_hbm.at[pl.ds(wide, 2 * HALO), :], rows.at[0 : 2 * HALO, :]),
        (fwd_hbm.at[pl.ds(thin, HALO), :], rows.at[2 * HALO : 3 * HALO, :]),
        (grad_hbm.at[pl.ds(thin, HALO), :], rows.at[3 * HALO : 4 * HALO, :]),
    )
    copies = [pltpu.make_async_copy(a, b, sems.at[i]) for i, (a, b) in enumerate(pairs)]
    for copy in copies:
        copy.start()
    for copy in copies:
        copy.wait()
    origin = lax.axis_index("z") * 2 * frames + side * frames
    fwd_len = lengths[plan[0, 0]]
    bwd_len = lengths[plan[0, 1]]
    gain_row = gain[...]
    for at, start, length in ((0, wide, bwd_len), (HALO, wide + HALO, bwd_len), (2 * HALO, thin, fwd_len)):
        value = conv_input(rows[at : at + HALO, :], gain_row, origin + start, length)
        mine, theirs = both(value, block, side == 0)
        to_far[at : at + HALO, :] = mine
        to_near[at : at + HALO, :] = theirs
    for part in range(2):
        at = (3 + part) * HALO
        value = rows[3 * HALO : 4 * HALO, part * half : (part + 1) * half]
        to_far[at : at + HALO, :] = value
        to_near[at : at + HALO, :] = value


def enter_kernel(
    block, plan_hbm, lengths_hbm, saved_hbm, fwd_hbm, gain_hbm, kernel_hbm,
    own, own_fwd, other, other_fwd, taps, plan, lengths, saved, fwd, gain, kernel, sems,
):
    frames = saved.shape[0]
    side = lax.axis_index("x")
    first = side == 0
    pairs = (
        (saved_hbm, saved),
        (kernel_hbm, kernel),
        (plan_hbm, plan),
        (lengths_hbm, lengths),
        (gain_hbm, gain),
        (fwd_hbm, fwd),
    )
    copies = [pltpu.make_async_copy(a, b, sems.at[i]) for i, (a, b) in enumerate(pairs)]
    for copy in copies:
        copy.start()
    for copy in copies[1:5]:
        copy.wait()
    taps[0:KW, :] = both(kernel[:, 0, :], block, first)[0]
    taps[KW : KW + 1, :] = jnp.zeros((1, taps.shape[1]), jnp.float32)
    origin = lax.axis_index("z") * 2 * frames
    fwd_len = lengths[plan[0, 0]]
    bwd_len = lengths[plan[0, 1]]
    gain_row = gain[...]

    def pass_over(source, mine_out, theirs_out, length):
        def body(i, carry):
            at = pl.multiple_of(i * ROWS, ROWS)
            start = origin + side * frames + at
            value = conv_input(source[pl.ds(at, ROWS), :], gain_row, start, length)
            mine, theirs = both(value, block, first)
            mine_out[pl.ds(at, ROWS), :] = mine
            theirs_out[pl.ds(at, ROWS), :] = theirs
            return carry

        lax.fori_loop(0, frames // ROWS, body, 0, unroll=4)

    copies[0].wait()
    pass_over(saved, own, other, bwd_len)
    copies[5].wait()
    pass_over(fwd, own_fwd, other_fwd, fwd_len)


def slide(buffer, chunk, start, count, weight):
    total = jnp.zeros((count, LANES), jnp.float32)
    for shift in range(8):
        tile = buffer[chunk, pl.ds(start + shift, count + 24), :]
        for step in range(4):
            offset = 8 * step + shift
            if 1 <= offset <= KW:
                total = total + weight(offset) * tile[8 * step : 8 * step + count]
    return total


def outside(near, far, rows, lanes, ahead):
    first = lax.axis_index("x") == 0
    return jnp.where(first == ahead, near[rows, lanes], far[rows, lanes])


def store_rows(buffer, chunk, row, values):
    if not isinstance(row, int):
        row = pl.multiple_of(row, 8)
    buffer[chunk, pl.ds(row, values.shape[0]), :] = values.astype(jnp.float32)


def fwd_kernel(own, got, taps, near, far, hidden_own, hidden_other, window):
    side = lax.axis_index("x")
    frames = own.shape[0]
    mine = side * frames
    theirs = frames - mine
    edge = slice(2 * HALO, 3 * HALO)

    def body(chunk, carry):
        lanes = pl.ds(pl.multiple_of(chunk * LANES, LANES), LANES)
        put = functools.partial(store_rows, window, 0)
        put(0, outside(near, far, edge, lanes, True))
        put(HALO + mine, own[:, lanes])
        put(HALO + theirs, got[:, lanes])
        put(HALO + 2 * frames, outside(near, far, edge, lanes, False))
        put(2 * HALO + 2 * frames, jnp.zeros((8, LANES), jnp.float32))

        def weight(offset):
            return taps[offset - 1 : offset, lanes]

        for half in range(2):
            mixed = slide(window, 0, half * frames, frames, weight)
            hidden = (mixed * jax.nn.sigmoid(mixed)).astype(jnp.bfloat16)

            @pl.when(side == half)
            def _():
                hidden_own[:, lanes] = hidden

            @pl.when(side != half)
            def _():
                hidden_other[:, lanes] = hidden

        return carry

    lax.fori_loop(0, own.shape[1] // LANES, body, 0, unroll=2)


def conv_kernel(
    factor, own, got, taps, grad_hbm, grad_got, near, far,
    *refs,
):
    blocks = refs[:-6]
    keep, grad_window, hidden_saved, window, product, sem = refs[-6:]
    side = lax.axis_index("x")
    frames = grad_got.shape[0]
    mine = side * frames
    spot = pl.ds(pl.multiple_of(HALO + mine, HALO), frames)
    copy = pltpu.make_async_copy(grad_hbm, grad_window.at[spot, :], sem)
    copy.start()
    theirs = frames - mine
    chunks = own.shape[1] // LANES
    half = own.shape[1]
    for part in range(2):
        rows = slice((3 + part) * HALO, (4 + part) * HALO)
        lanes = slice(part * half, (part + 1) * half)
        grad_window[0:HALO, lanes] = outside(near, far, rows, slice(None), True)
        grad_window[HALO + 2 * frames :, lanes] = outside(near, far, rows, slice(None), False)
    grad_window[pl.ds(pl.multiple_of(HALO + theirs, HALO), frames), :] = grad_got[...]
    edge = slice(0, 2 * HALO)

    def body(chunk, carry):
        lanes = pl.ds(pl.multiple_of(chunk * LANES, LANES), LANES)

        put = functools.partial(store_rows, window, 0)
        put(0, outside(near, far, edge, lanes, True))
        put(2 * HALO + mine, own[:, lanes])
        put(2 * HALO + theirs, got[:, lanes])
        put(2 * HALO + 2 * frames, outside(near, far, edge, lanes, False))
        put(4 * HALO + 2 * frames, jnp.zeros((8, LANES), jnp.float32))

        def weight(offset):
            return taps[offset - 1 : offset, lanes]

        keep[2 * frames + 2 * HALO :, lanes] = window[0, 0 : 2 * frames + 4 * HALO, :].astype(jnp.bfloat16)
        span = frames + HALO
        for half in range(2):
            mixed = slide(window, 0, half * span, span, weight)
            gate = jax.nn.sigmoid(mixed)
            hidden = mixed * gate
            value = gate + hidden * (1.0 - gate)
            keep[pl.ds(half * span, span), lanes] = value.astype(jnp.bfloat16)
            inner = hidden[HALO:] if half == 0 else hidden[:frames]
            hidden_saved[pl.ds(half * frames, frames), lanes] = inner.astype(jnp.bfloat16)
        return carry

    lax.fori_loop(0, chunks, body, 0, unroll=2)
    copy.wait()
    depth = len(blocks)
    here = lax.axis_index("z")

    def outer(index, carry):
        lanes = pl.ds(pl.multiple_of(index * 6 * LANES, 6 * LANES), 6 * LANES)
        value = lax.dot_general(
            hidden_saved[...],
            grad_window[HALO : HALO + 2 * frames, lanes],
            (((0,), (0,)), ((), ())),
            preferred_element_type=jnp.float32,
        )
        value = (value * factor).astype(jnp.bfloat16)
        product[...] = value.reshape(product.shape)
        for k, out in enumerate(blocks):
            place = jnp.where(here + k < depth, here + k, here + k - depth)
            out[:, lanes] = product[place]
        return carry

    lax.fori_loop(0, grad_window.shape[1] // (6 * LANES), outer, 0)


def back_kernel(
    factor, places, plan, lengths, grad_window, kept, taps, *refs
):
    blocks, (grad_own, grad_other, kernel_grad, weights, conv_grad, inputs) = refs[:-6], refs[-6:]
    rows = blocks[0].shape[0]
    depth = weights.shape[0] // rows
    for block, (step, offset, count) in zip(blocks, places):
        place = lax.axis_index("z") + step
        place = jnp.where(place < depth, place, place - depth) * rows + offset
        weights[pl.ds(pl.multiple_of(place, ROWS), count), :] = block[0:count, :]
    side = lax.axis_index("x")
    frames = grad_own.shape[0]
    chunks = taps.shape[1] // LANES
    origin = lax.axis_index("z") * 2 * frames
    bwd_len = lengths[plan[0, 1]]

    def product(index, carry):
        lanes = pl.ds(pl.multiple_of(index * 2 * LANES, 2 * LANES), 2 * LANES)
        hidden_grad = lax.dot_general(
            grad_window[...],
            weights[lanes, :],
            (((1,), (1,)), ((), ())),
            preferred_element_type=jnp.float32,
        )
        value = (hidden_grad * kept[0 : 2 * frames + 2 * HALO, lanes].astype(jnp.float32)).astype(jnp.bfloat16).astype(jnp.float32)
        for part in range(2):
            chunk = 2 * index + part
            conv_grad[chunk, 0 : 2 * frames + 2 * HALO, :] = value[:, part * LANES : (part + 1) * LANES]
            conv_grad[chunk, 2 * frames + 2 * HALO :, :] = jnp.zeros((8, LANES), jnp.float32)
        return carry

    lax.fori_loop(0, chunks // 2, product, 0)

    def body(chunk, carry):
        lanes = pl.ds(pl.multiple_of(chunk * LANES, LANES), LANES)

        size = 2 * frames + 4 * HALO
        inputs[0, 0:size, :] = kept[2 * frames + 2 * HALO :, lanes].astype(jnp.float32)
        inputs[0, size:, :] = jnp.zeros((8, LANES), jnp.float32)

        def weight(offset):
            return taps[KW - offset : KW - offset + 1, lanes]

        for half in range(2):
            total = slide(conv_grad, chunk, half * frames, frames, weight)
            frame = origin + half * frames + lax.broadcasted_iota(jnp.int32, (frames, 1), 0)
            total = (total * (frame < bwd_len).astype(jnp.float32)).astype(jnp.bfloat16)

            @pl.when(side == half)
            def _():
                grad_own[:, lanes] = total

            @pl.when(side != half)
            def _():
                grad_other[:, lanes] = total

        for shift in range(8):
            sums = [jnp.zeros((8, LANES), jnp.float32) for _ in range(4)]
            for half in range(2):
                left = conv_grad[chunk, pl.ds(HALO + half * frames, frames), :]
                right = inputs[0, pl.ds(HALO + half * frames + shift, frames + 24), :]
                for step in range(4):
                    if 1 <= 8 * step + shift <= KW:
                        term = left * right[8 * step : 8 * step + frames]
                        sums[step] = sums[step] + jnp.sum(term.reshape(frames // 8, 8, LANES), axis=0)
            for step in range(4):
                tap = 8 * step + shift - 1
                if 0 <= tap < KW:
                    row = jnp.sum(sums[step], axis=0, keepdims=True) * factor
                    kernel_grad[tap : tap + 1, lanes] = row
        kernel_grad[KW : KW + 1, lanes] = jnp.zeros((1, LANES), jnp.float32)
        return carry

    lax.fori_loop(0, chunks, body, 0, unroll=2)


def leave_kernel(block, own, got, saved, grad, gain, out):
    first = lax.axis_index("x") == 0
    gain_row = gain[...]

    def body(i, carry):
        at = pl.ds(pl.multiple_of(i * ROWS, ROWS), ROWS)
        mine, theirs = own[at, :], got[at, :]
        even, odd = jnp.where(first, mine, theirs), jnp.where(first, theirs, mine)
        hat_grad = unite(even, odd, block).astype(jnp.float32) * gain_row
        hat, inverse = normalize(saved[at, :].astype(jnp.float32))
        back = grad[at, :].astype(jnp.float32) + inverse * (
            hat_grad
            - jnp.mean(hat_grad, axis=-1, keepdims=True)
            - hat * jnp.mean(hat_grad * hat, axis=-1, keepdims=True)
        )
        out[at, :] = back.astype(jnp.bfloat16)
        return carry

    lax.fori_loop(0, saved.shape[0] // ROWS, body, 0, unroll=4)


def totals_kernel(block, own, got, kernel, gain, kernel_out, gain_out):
    first = lax.axis_index("x") == 0
    mine, theirs = own[...], got[...]
    even, odd = jnp.where(first, mine, theirs), jnp.where(first, theirs, mine)
    total = unite(even.astype(jnp.float32), odd.astype(jnp.float32), block)[:KW]
    kernel_out[:, 0, :] = total
    gain_out[...] = jnp.sum(kernel[:, 0, :] * total, axis=0, keepdims=True) / gain[...]


def relay_kernel(source, out):
    out[...] = source[...]


def finish_kernel(first, second, third, out):
    out[...] = first[...].astype(jnp.float32) + second[...].astype(jnp.float32) + third[...].astype(jnp.float32)


def per_device(fwd_input, saved_input, grad_in, gain, kernel, w_out, lengths, plan):
    frames, width = fwd_input.shape[1:]
    depth = lax.axis_size("z")
    rows = w_out.shape[1]
    half = rows * depth
    pair = 2 * frames
    factor = float(pair * depth) ** (-0.5)
    fwd_rows = fwd_input[0]
    saved_rows = saved_input[0]
    upstream = grad_in[0]
    bf16, f32 = jnp.bfloat16, jnp.float32

    barrier = lax.optimization_barrier

    up = [(i, (i + 1) % depth) for i in range(depth)]
    down = [(j, i) for i, j in up]

    def ring(pair_of):
        return lax.ppermute(pair_of[0], "z", up), lax.ppermute(pair_of[1], "z", down)

    grad_got = partner(upstream)
    to_near, to_far = call(
        functools.partial(edge_kernel, rows),
        [((5 * HALO, half), bf16)] * 2,
        [HBM] * 6,
        [
            pltpu.SMEM(plan.shape, jnp.int32),
            pltpu.SMEM(lengths.shape, jnp.int32),
            pltpu.VMEM(gain.shape, f32),
            pltpu.VMEM((4 * HALO, width), bf16),
            pltpu.SemaphoreType.DMA((6,)),
        ],
        limit=None,
        size=16 * HALO * width,
    )(plan, lengths, saved_rows, fwd_rows, upstream, gain)
    count = 2 * depth
    tm = ("z", "x")
    hops = [(t, t + 1 if t % 2 else t - 1) for t in range(count)]
    near = lax.ppermute(to_near, tm, [(a, b) for a, b in hops if 0 <= b < count])
    hops = [(t, t + 2 if t % 2 else t - 2) for t in range(count)]
    far = lax.ppermute(to_far, tm, [(a, b) for a, b in hops if 0 <= b < count])

    block = w_out[0]
    round_1 = ring((block, block))
    tap_rows = jnp.transpose(kernel, (1, 0, 2))

    own, own_fwd, other, other_fwd, taps = call(
        functools.partial(enter_kernel, rows),
        [((frames, half), bf16)] * 4 + [((KW + 1, half), f32)],
        [HBM] * 6,
        [
            pltpu.SMEM(plan.shape, jnp.int32),
            pltpu.SMEM(lengths.shape, jnp.int32),
            pltpu.VMEM((frames, width), bf16),
            pltpu.VMEM((frames, width), bf16),
            pltpu.VMEM(gain.shape, f32),
            pltpu.VMEM(tap_rows.shape, f32),
            pltpu.SemaphoreType.DMA((6,)),
        ],
        limit=None,
        flops=12 * 2 * frames * width,
        size=10 * frames * width,
    )(plan, lengths, saved_rows, fwd_rows, gain, tap_rows)
    got = partner(other)
    got_fwd = partner(other_fwd)
    round_2 = ring(round_1)
    round_3 = ring(round_2)
    *partial, kept, grad_window = call(
        functools.partial(conv_kernel, factor),
        [
            *[((rows, width), bf16)] * depth,
            ((2 * pair + 6 * HALO, half), bf16),
            ((pair + 2 * HALO, width), bf16),
        ],
        [VMEM] * 3 + [HBM] + [VMEM] * 3,
        [
            pltpu.VMEM((pair, half), bf16),
            pltpu.VMEM((1, pair + 4 * HALO + 8, LANES), f32),
            pltpu.VMEM((depth, rows, 6 * LANES), bf16),
            pltpu.SemaphoreType.DMA(()),
        ],
        limit=None,
        flops=2 * KW * 2 * pair * half,
        size=16 * pair * half,
    )(own, got, taps, upstream, grad_got, near, far)

    hidden_own, hidden_other = call(
        fwd_kernel,
        [((frames, half), bf16)] * 2,
        [VMEM] * 5,
        [pltpu.VMEM((1, pair + 2 * HALO + 8, LANES), f32)],
        limit=None,
        flops=2 * KW * pair * half,
        size=8 * pair * half,
    )(own_fwd, got_fwd, taps, near, far)
    partial, round_3 = barrier((partial, round_3))

    def plus(arrived, own_part):
        return (arrived.astype(f32) + own_part.astype(f32)).astype(bf16)

    round_4 = lax.ppermute(round_3[0], "z", up)
    back_1 = lax.ppermute(partial[depth // 2], "z", down)
    blocks = [block]
    places = [(0, 0, rows)]
    for k, (behind, ahead) in enumerate((round_1, round_2, round_3), 1):
        blocks += [behind, ahead]
        places += [(depth - k, 0, rows), (k, 0, rows)]
    blocks += [round_4]
    places += [(depth // 2, 0, rows)]
    back_2 = ring((partial[depth // 2 - 1], plus(back_1, partial[depth // 2 + 1])))
    norm_own, norm_other, kernel_local, w_half = call(
        functools.partial(back_kernel, factor, tuple(places)),
        [
            ((frames, half), bf16),
            ((frames, half), bf16),
            ((KW + 1, half), f32),
            ((half, width), bf16),
        ],
        [SMEM, SMEM] + [VMEM] * (3 + len(blocks)),
        [
            pltpu.VMEM((half // LANES, pair + 2 * HALO + 8, LANES), f32),
            pltpu.VMEM((1, pair + 4 * HALO + 8, LANES), f32),
        ],
        flops=4 * KW * pair * half,
        size=12 * pair * half,
        limit=40<<20,
    )(plan, lengths, grad_window, kept, taps, *blocks)
    norm_got = partner(norm_other)
    total = kernel_local.astype(bf16)
    step = 1
    while step < depth:
        arrived = lax.ppermute(total, "z", [(i, i ^ step) for i in range(depth)])
        total = (total.astype(f32) + arrived.astype(f32)).astype(bf16)
        step *= 2
    total_got = partner(total)

    back_3 = ring((plus(back_2[0], partial[2]), plus(back_2[1], partial[-2])))
    back_4 = ring((plus(back_3[0], partial[1]), plus(back_3[1], partial[-1])))
    (weight_grad,) = call(
        finish_kernel, [((rows, width), f32)], [VMEM] * 3, size=10 * rows * width
    )(back_4[0], back_4[1], partial[0])

    product = jnp.dot(hidden_other, w_half, preferred_element_type=f32).astype(bf16)
    product_got = partner(product)
    output = (
        fwd_rows.astype(f32)
        + (jnp.dot(hidden_own, w_half, preferred_element_type=f32) + product_got.astype(f32))
    ).astype(bf16)
    passed_activation = from_behind(output[None], 1)

    (input_back,) = call(
        functools.partial(leave_kernel, rows),
        [((frames, width), bf16)],
        [VMEM] * 5,
        flops=20 * frames * width,
        size=8 * frames * width,
    )(norm_own, norm_got, saved_rows, upstream, gain)
    passed_gradient = from_behind(input_back[None], -1)
    kernel_grad, gain_grad = call(
        functools.partial(totals_kernel, rows),
        [((KW, 1, width), f32), ((1, width), f32)],
        [VMEM] * 4,
        limit=40<<20,
        flops=4 * KW * width,
        size=12 * KW * width,
    )(total, total_got, tap_rows, gain)
    (passed_gradient,) = call(
        relay_kernel, [(passed_gradient.shape, bf16)], [VMEM], size=4 * frames * width
    )(passed_gradient)
    return (
        passed_activation,
        passed_gradient,
        weight_grad[None],
        jnp.transpose(kernel_grad, (1, 0, 2)),
        gain_grad,
    )


def solution(mesh):
    sections, pieces = mesh.devices.shape
    folded = Mesh(mesh.devices.reshape(sections, pieces // 2, 2), ("section", "z", "x"))
    split = P("section", ("z", "x"), None)
    placed = (
        split,
        split,
        split,
        P("section", None),
        P("section", None, None),
        split,
        P(),
        P("section", None),
    )

    return jax.shard_map(
        per_device,
        mesh=folded,
        in_specs=placed,
        out_specs=(split, split, split, P("section", None, None), P("section", None)),
        check_vma=False,
    )
```

```python
import functools

import jax
import jax.numpy as jnp
from jax import lax
from jax.experimental import pallas as pl
from jax.experimental.pallas import tpu as pltpu
from jax.sharding import Mesh
from jax.sharding import PartitionSpec as P


KW = 31
HALO = 16
LANES = 128
ROWS = 16


VMEM = pl.BlockSpec(memory_space=pltpu.VMEM)
SMEM = pl.BlockSpec(memory_space=pltpu.SMEM)
HBM = pl.BlockSpec(memory_space=pltpu.HBM)


def call(body, outs, in_specs, scratch=(), flops=0, size=0, limit=40 << 20):
    return pl.pallas_call(
        body,
        out_shape=[jax.ShapeDtypeStruct(shape, kind) for shape, kind in outs],
        in_specs=in_specs,
        out_specs=[VMEM] * len(outs),
        scratch_shapes=list(scratch),
        compiler_params=pltpu.CompilerParams(vmem_limit_bytes=limit),
        cost_estimate=pl.CostEstimate(flops=flops, bytes_accessed=size, transcendentals=0),
    )


def partner(array):
    return lax.ppermute(array, "x", [(0, 1), (1, 0)])


def from_behind(array, by):
    length = lax.axis_size("section")
    pairs = [(i, i + by) for i in range(length) if 0 <= i + by < length]
    return lax.ppermute(array, "section", pairs)


def divide(array, block):
    count = array.shape[1] // block
    pieces = [array[:, k * block : (k + 1) * block] for k in range(count)]
    return jnp.concatenate(pieces[0::2], axis=1), jnp.concatenate(pieces[1::2], axis=1)


def unite(even, odd, block):
    pieces = []
    for k in range(even.shape[1] // block):
        pieces += [even[:, k * block : (k + 1) * block], odd[:, k * block : (k + 1) * block]]
    return jnp.concatenate(pieces, axis=1)


def normalize(values):
    center = values - jnp.mean(values, axis=-1, keepdims=True)
    inverse = lax.rsqrt(jnp.mean(center * center, axis=-1, keepdims=True) + 1e-05)
    return (center * inverse, inverse)


def mask_of(start, length):
    return ((start + lax.broadcasted_iota(jnp.int32, (ROWS, 1), 0)) < length).astype(jnp.float32)


def conv_input(rows, gain_row, start, length):
    hat, _ = normalize(rows.astype(jnp.float32))
    return (hat * gain_row * mask_of(start, length)).astype(jnp.bfloat16)


def both(array, block, first):
    even, odd = divide(array, block)
    return jnp.where(first, even, odd), jnp.where(first, odd, even)


def edge_kernel(
    block, plan_hbm, lengths_hbm, saved_hbm, fwd_hbm, grad_hbm, gain_hbm,
    to_near, to_far, plan, lengths, gain, rows, sems,
):
    frames = saved_hbm.shape[0]
    half = to_near.shape[1]
    side = lax.axis_index("x")
    wide = pl.multiple_of(side * (frames - 2 * HALO), HALO)
    thin = pl.multiple_of(side * (frames - HALO), HALO)
    pairs = (
        (plan_hbm, plan),
        (lengths_hbm, lengths),
        (gain_hbm, gain),
        (saved_hbm.at[pl.ds(wide, 2 * HALO), :], rows.at[0 : 2 * HALO, :]),
        (fwd_hbm.at[pl.ds(thin, HALO), :], rows.at[2 * HALO : 3 * HALO, :]),
        (grad_hbm.at[pl.ds(thin, HALO), :], rows.at[3 * HALO : 4 * HALO, :]),
    )
    copies = [pltpu.make_async_copy(a, b, sems.at[i]) for i, (a, b) in enumerate(pairs)]
    for copy in copies:
        copy.start()
    for copy in copies:
        copy.wait()
    origin = lax.axis_index("z") * 2 * frames + side * frames
    fwd_len = lengths[plan[0, 0]]
    bwd_len = lengths[plan[0, 1]]
    gain_row = gain[...]
    for at, start, length in ((0, wide, bwd_len), (HALO, wide + HALO, bwd_len), (2 * HALO, thin, fwd_len)):
        value = conv_input(rows[at : at + HALO, :], gain_row, origin + start, length)
        mine, theirs = both(value, block, side == 0)
        to_far[at : at + HALO, :] = mine
        to_near[at : at + HALO, :] = theirs
    for part in range(2):
        at = (3 + part) * HALO
        value = rows[3 * HALO : 4 * HALO, part * half : (part + 1) * half]
        to_far[at : at + HALO, :] = value
        to_near[at : at + HALO, :] = value


def enter_kernel(
    block, plan_hbm, lengths_hbm, saved_hbm, fwd_hbm, gain_hbm, kernel_hbm,
    own, own_fwd, other, other_fwd, taps, plan, lengths, saved, fwd, gain, kernel, sems,
):
    frames = saved.shape[0]
    side = lax.axis_index("x")
    first = side == 0
    pairs = (
        (saved_hbm, saved),
        (kernel_hbm, kernel),
        (plan_hbm, plan),
        (lengths_hbm, lengths),
        (gain_hbm, gain),
        (fwd_hbm, fwd),
    )
    copies = [pltpu.make_async_copy(a, b, sems.at[i]) for i, (a, b) in enumerate(pairs)]
    for copy in copies:
        copy.start()
    for copy in copies[1:5]:
        copy.wait()
    taps[0:KW, :] = both(kernel[:, 0, :], block, first)[0]
    taps[KW : KW + 1, :] = jnp.zeros((1, taps.shape[1]), jnp.float32)
    origin = lax.axis_index("z") * 2 * frames
    fwd_len = lengths[plan[0, 0]]
    bwd_len = lengths[plan[0, 1]]
    gain_row = gain[...]

    def pass_over(source, mine_out, theirs_out, length):
        def body(i, carry):
            at = pl.multiple_of(i * ROWS, ROWS)
            start = origin + side * frames + at
            value = conv_input(source[pl.ds(at, ROWS), :], gain_row, start, length)
            mine, theirs = both(value, block, first)
            mine_out[pl.ds(at, ROWS), :] = mine
            theirs_out[pl.ds(at, ROWS), :] = theirs
            return carry

        lax.fori_loop(0, frames // ROWS, body, 0, unroll=8)

    copies[0].wait()
    pass_over(saved, own, other, bwd_len)
    copies[5].wait()
    pass_over(fwd, own_fwd, other_fwd, fwd_len)


def slide(buffer, chunk, start, count, weight):
    total = jnp.zeros((count, LANES), jnp.float32)
    for shift in range(8):
        tile = buffer[chunk, pl.ds(start + shift, count + 24), :]
        for step in range(4):
            offset = 8 * step + shift
            if 1 <= offset <= KW:
                total = total + weight(offset) * tile[8 * step : 8 * step + count]
    return total


def outside(near, far, rows, lanes, ahead):
    first = lax.axis_index("x") == 0
    return jnp.where(first == ahead, near[rows, lanes], far[rows, lanes])


def store_rows(buffer, chunk, row, values):
    if not isinstance(row, int):
        row = pl.multiple_of(row, 8)
    buffer[chunk, pl.ds(row, values.shape[0]), :] = values.astype(jnp.float32)


def fwd_kernel(own, got, taps, near, far, hidden_own, hidden_other, window):
    side = lax.axis_index("x")
    frames = own.shape[0]
    mine = side * frames
    theirs = frames - mine
    edge = slice(2 * HALO, 3 * HALO)

    def body(chunk, carry):
        lanes = pl.ds(pl.multiple_of(chunk * LANES, LANES), LANES)
        put = functools.partial(store_rows, window, 0)
        put(0, outside(near, far, edge, lanes, True))
        put(HALO + mine, own[:, lanes])
        put(HALO + theirs, got[:, lanes])
        put(HALO + 2 * frames, outside(near, far, edge, lanes, False))
        put(2 * HALO + 2 * frames, jnp.zeros((8, LANES), jnp.float32))

        def weight(offset):
            return taps[offset - 1 : offset, lanes]

        for half in range(2):
            mixed = slide(window, 0, half * frames, frames, weight)
            hidden = (mixed * jax.nn.sigmoid(mixed)).astype(jnp.bfloat16)

            @pl.when(side == half)
            def _():
                hidden_own[:, lanes] = hidden

            @pl.when(side != half)
            def _():
                hidden_other[:, lanes] = hidden

        return carry

    lax.fori_loop(0, own.shape[1] // LANES, body, 0, unroll=3)


def conv_kernel(
    factor, own, got, taps, grad_hbm, grad_got, near, far,
    *refs,
):
    blocks = refs[:-6]
    keep, grad_window, hidden_saved, window, product, sem = refs[-6:]
    side = lax.axis_index("x")
    frames = grad_got.shape[0]
    mine = side * frames
    spot = pl.ds(pl.multiple_of(HALO + mine, HALO), frames)
    copy = pltpu.make_async_copy(grad_hbm, grad_window.at[spot, :], sem)
    copy.start()
    theirs = frames - mine
    chunks = own.shape[1] // LANES
    half = own.shape[1]
    for part in range(2):
        rows = slice((3 + part) * HALO, (4 + part) * HALO)
        lanes = slice(part * half, (part + 1) * half)
        grad_window[0:HALO, lanes] = outside(near, far, rows, slice(None), True)
        grad_window[HALO + 2 * frames :, lanes] = outside(near, far, rows, slice(None), False)
    grad_window[pl.ds(pl.multiple_of(HALO + theirs, HALO), frames), :] = grad_got[...]
    edge = slice(0, 2 * HALO)

    def body(chunk, carry):
        lanes = pl.ds(pl.multiple_of(chunk * LANES, LANES), LANES)

        put = functools.partial(store_rows, window, 0)
        put(0, outside(near, far, edge, lanes, True))
        put(2 * HALO + mine, own[:, lanes])
        put(2 * HALO + theirs, got[:, lanes])
        put(2 * HALO + 2 * frames, outside(near, far, edge, lanes, False))
        put(4 * HALO + 2 * frames, jnp.zeros((8, LANES), jnp.float32))

        def weight(offset):
            return taps[offset - 1 : offset, lanes]

        keep[2 * frames + 2 * HALO :, lanes] = window[0, 0 : 2 * frames + 4 * HALO, :].astype(jnp.bfloat16)
        span = frames + HALO
        for half in range(2):
            mixed = slide(window, 0, half * span, span, weight)
            gate = jax.nn.sigmoid(mixed)
            hidden = mixed * gate
            value = gate + hidden * (1.0 - gate)
            keep[pl.ds(half * span, span), lanes] = value.astype(jnp.bfloat16)
            inner = hidden[HALO:] if half == 0 else hidden[:frames]
            hidden_saved[pl.ds(half * frames, frames), lanes] = inner.astype(jnp.bfloat16)
        return carry

    lax.fori_loop(0, chunks, body, 0, unroll=3)
    copy.wait()
    depth = len(blocks)
    here = lax.axis_index("z")

    def outer(index, carry):
        lanes = pl.ds(pl.multiple_of(index * 6 * LANES, 6 * LANES), 6 * LANES)
        value = lax.dot_general(
            hidden_saved[...],
            grad_window[HALO : HALO + 2 * frames, lanes],
            (((0,), (0,)), ((), ())),
            preferred_element_type=jnp.float32,
        )
        value = (value * factor).astype(jnp.bfloat16)
        product[...] = value.reshape(product.shape)
        for k, out in enumerate(blocks):
            place = jnp.where(here + k < depth, here + k, here + k - depth)
            out[:, lanes] = product[place]
        return carry

    lax.fori_loop(0, grad_window.shape[1] // (6 * LANES), outer, 0)


def back_kernel(
    factor, places, plan, lengths, grad_window, kept, taps, *refs
):
    blocks, (grad_own, grad_other, kernel_grad, weights, conv_grad, inputs) = refs[:-6], refs[-6:]
    rows = blocks[0].shape[0]
    depth = weights.shape[0] // rows
    for block, (step, offset, count) in zip(blocks, places):
        place = lax.axis_index("z") + step
        place = jnp.where(place < depth, place, place - depth) * rows + offset
        weights[pl.ds(pl.multiple_of(place, ROWS), count), :] = block[0:count, :]
    side = lax.axis_index("x")
    frames = grad_own.shape[0]
    chunks = taps.shape[1] // LANES
    origin = lax.axis_index("z") * 2 * frames
    bwd_len = lengths[plan[0, 1]]

    def product(index, carry):
        lanes = pl.ds(pl.multiple_of(index * 2 * LANES, 2 * LANES), 2 * LANES)
        hidden_grad = lax.dot_general(
            grad_window[...],
            weights[lanes, :],
            (((1,), (1,)), ((), ())),
            preferred_element_type=jnp.float32,
        )
        value = (hidden_grad * kept[0 : 2 * frames + 2 * HALO, lanes].astype(jnp.float32)).astype(jnp.bfloat16).astype(jnp.float32)
        for part in range(2):
            chunk = 2 * index + part
            conv_grad[chunk, 0 : 2 * frames + 2 * HALO, :] = value[:, part * LANES : (part + 1) * LANES]
            conv_grad[chunk, 2 * frames + 2 * HALO :, :] = jnp.zeros((8, LANES), jnp.float32)
        return carry

    lax.fori_loop(0, chunks // 2, product, 0)

    def body(chunk, carry):
        lanes = pl.ds(pl.multiple_of(chunk * LANES, LANES), LANES)

        size = 2 * frames + 4 * HALO
        inputs[0, 0:size, :] = kept[2 * frames + 2 * HALO :, lanes].astype(jnp.float32)
        inputs[0, size:, :] = jnp.zeros((8, LANES), jnp.float32)

        def weight(offset):
            return taps[KW - offset : KW - offset + 1, lanes]

        for half in range(2):
            total = slide(conv_grad, chunk, half * frames, frames, weight)
            frame = origin + half * frames + lax.broadcasted_iota(jnp.int32, (frames, 1), 0)
            total = (total * (frame < bwd_len).astype(jnp.float32)).astype(jnp.bfloat16)

            @pl.when(side == half)
            def _():
                grad_own[:, lanes] = total

            @pl.when(side != half)
            def _():
                grad_other[:, lanes] = total

        for shift in range(8):
            sums = [jnp.zeros((8, LANES), jnp.float32) for _ in range(4)]
            for half in range(2):
                left = conv_grad[chunk, pl.ds(HALO + half * frames, frames), :]
                right = inputs[0, pl.ds(HALO + half * frames + shift, frames + 24), :]
                for step in range(4):
                    if 1 <= 8 * step + shift <= KW:
                        term = left * right[8 * step : 8 * step + frames]
                        sums[step] = sums[step] + jnp.sum(term.reshape(frames // 8, 8, LANES), axis=0)
            for step in range(4):
                tap = 8 * step + shift - 1
                if 0 <= tap < KW:
                    row = jnp.sum(sums[step], axis=0, keepdims=True) * factor
                    kernel_grad[tap : tap + 1, lanes] = row
        kernel_grad[KW : KW + 1, lanes] = jnp.zeros((1, LANES), jnp.float32)
        return carry

    lax.fori_loop(0, chunks, body, 0, unroll=3)


def leave_kernel(block, own, got, saved, grad, gain, out):
    first = lax.axis_index("x") == 0
    gain_row = gain[...]

    def body(i, carry):
        at = pl.ds(pl.multiple_of(i * ROWS, ROWS), ROWS)
        mine, theirs = own[at, :], got[at, :]
        even, odd = jnp.where(first, mine, theirs), jnp.where(first, theirs, mine)
        hat_grad = unite(even, odd, block).astype(jnp.float32) * gain_row
        hat, inverse = normalize(saved[at, :].astype(jnp.float32))
        back = grad[at, :].astype(jnp.float32) + inverse * (
            hat_grad
            - jnp.mean(hat_grad, axis=-1, keepdims=True)
            - hat * jnp.mean(hat_grad * hat, axis=-1, keepdims=True)
        )
        out[at, :] = back.astype(jnp.bfloat16)
        return carry

    lax.fori_loop(0, saved.shape[0] // ROWS, body, 0, unroll=8)


def totals_kernel(block, own, got, kernel, gain, kernel_out, gain_out):
    first = lax.axis_index("x") == 0
    mine, theirs = own[...], got[...]
    even, odd = jnp.where(first, mine, theirs), jnp.where(first, theirs, mine)
    total = unite(even.astype(jnp.float32), odd.astype(jnp.float32), block)[:KW]
    kernel_out[:, 0, :] = total
    gain_out[...] = jnp.sum(kernel[:, 0, :] * total, axis=0, keepdims=True) / gain[...]


def relay_kernel(source, out):
    out[...] = source[...]


def finish_kernel(first, second, third, out):
    out[...] = first[...].astype(jnp.float32) + second[...].astype(jnp.float32) + third[...].astype(jnp.float32)


def per_device(fwd_input, saved_input, grad_in, gain, kernel, w_out, lengths, plan):
    frames, width = fwd_input.shape[1:]
    depth = lax.axis_size("z")
    rows = w_out.shape[1]
    half = rows * depth
    pair = 2 * frames
    factor = float(pair * depth) ** (-0.5)
    fwd_rows = fwd_input[0]
    saved_rows = saved_input[0]
    upstream = grad_in[0]
    bf16, f32 = jnp.bfloat16, jnp.float32

    barrier = lax.optimization_barrier

    up = [(i, (i + 1) % depth) for i in range(depth)]
    down = [(j, i) for i, j in up]

    def ring(pair_of):
        return lax.ppermute(pair_of[0], "z", up), lax.ppermute(pair_of[1], "z", down)

    grad_got = partner(upstream)
    to_near, to_far = call(
        functools.partial(edge_kernel, rows),
        [((5 * HALO, half), bf16)] * 2,
        [HBM] * 6,
        [
            pltpu.SMEM(plan.shape, jnp.int32),
            pltpu.SMEM(lengths.shape, jnp.int32),
            pltpu.VMEM(gain.shape, f32),
            pltpu.VMEM((4 * HALO, width), bf16),
            pltpu.SemaphoreType.DMA((6,)),
        ],
        limit=None,
        size=16 * HALO * width,
    )(plan, lengths, saved_rows, fwd_rows, upstream, gain)
    count = 2 * depth
    tm = ("z", "x")
    hops = [(t, t + 1 if t % 2 else t - 1) for t in range(count)]
    near = lax.ppermute(to_near, tm, [(a, b) for a, b in hops if 0 <= b < count])
    hops = [(t, t + 2 if t % 2 else t - 2) for t in range(count)]
    far = lax.ppermute(to_far, tm, [(a, b) for a, b in hops if 0 <= b < count])

    block = w_out[0]
    round_1 = ring((block, block))
    tap_rows = jnp.transpose(kernel, (1, 0, 2))

    own, own_fwd, other, other_fwd, taps = call(
        functools.partial(enter_kernel, rows),
        [((frames, half), bf16)] * 4 + [((KW + 1, half), f32)],
        [HBM] * 6,
        [
            pltpu.SMEM(plan.shape, jnp.int32),
            pltpu.SMEM(lengths.shape, jnp.int32),
            pltpu.VMEM((frames, width), bf16),
            pltpu.VMEM((frames, width), bf16),
            pltpu.VMEM(gain.shape, f32),
            pltpu.VMEM(tap_rows.shape, f32),
            pltpu.SemaphoreType.DMA((6,)),
        ],
        limit=None,
        flops=12 * 2 * frames * width,
        size=10 * frames * width,
    )(plan, lengths, saved_rows, fwd_rows, gain, tap_rows)
    got = partner(other)
    got_fwd = partner(other_fwd)
    round_2 = ring(round_1)
    round_3 = ring(round_2)
    *partial, kept, grad_window = call(
        functools.partial(conv_kernel, factor),
        [
            *[((rows, width), bf16)] * depth,
            ((2 * pair + 6 * HALO, half), bf16),
            ((pair + 2 * HALO, width), bf16),
        ],
        [VMEM] * 3 + [HBM] + [VMEM] * 3,
        [
            pltpu.VMEM((pair, half), bf16),
            pltpu.VMEM((1, pair + 4 * HALO + 8, LANES), f32),
            pltpu.VMEM((depth, rows, 6 * LANES), bf16),
            pltpu.SemaphoreType.DMA(()),
        ],
        limit=None,
        flops=2 * KW * 2 * pair * half,
        size=16 * pair * half,
    )(own, got, taps, upstream, grad_got, near, far)

    hidden_own, hidden_other = call(
        fwd_kernel,
        [((frames, half), bf16)] * 2,
        [VMEM] * 5,
        [pltpu.VMEM((1, pair + 2 * HALO + 8, LANES), f32)],
        limit=None,
        flops=2 * KW * pair * half,
        size=8 * pair * half,
    )(own_fwd, got_fwd, taps, near, far)
    partial, round_3 = barrier((partial, round_3))

    def plus(arrived, own_part):
        return (arrived.astype(f32) + own_part.astype(f32)).astype(bf16)

    round_4 = lax.ppermute(round_3[0], "z", up)
    back_1 = lax.ppermute(partial[depth // 2], "z", down)
    blocks = [block]
    places = [(0, 0, rows)]
    for k, (behind, ahead) in enumerate((round_1, round_2, round_3), 1):
        blocks += [behind, ahead]
        places += [(depth - k, 0, rows), (k, 0, rows)]
    blocks += [round_4]
    places += [(depth // 2, 0, rows)]
    back_2 = ring((partial[depth // 2 - 1], plus(back_1, partial[depth // 2 + 1])))
    norm_own, norm_other, kernel_local, w_half = call(
        functools.partial(back_kernel, factor, tuple(places)),
        [
            ((frames, half), bf16),
            ((frames, half), bf16),
            ((KW + 1, half), f32),
            ((half, width), bf16),
        ],
        [SMEM, SMEM] + [VMEM] * (3 + len(blocks)),
        [
            pltpu.VMEM((half // LANES, pair + 2 * HALO + 8, LANES), f32),
            pltpu.VMEM((1, pair + 4 * HALO + 8, LANES), f32),
        ],
        flops=4 * KW * pair * half,
        size=12 * pair * half,
        limit=40<<20,
    )(plan, lengths, grad_window, kept, taps, *blocks)
    norm_got = partner(norm_other)
    total = kernel_local.astype(bf16)
    step = 1
    while step < depth:
        arrived = lax.ppermute(total, "z", [(i, i ^ step) for i in range(depth)])
        total = (total.astype(f32) + arrived.astype(f32)).astype(bf16)
        step *= 2
    total_got = partner(total)

    back_3 = ring((plus(back_2[0], partial[2]), plus(back_2[1], partial[-2])))
    back_4 = ring((plus(back_3[0], partial[1]), plus(back_3[1], partial[-1])))
    (weight_grad,) = call(
        finish_kernel, [((rows, width), f32)], [VMEM] * 3, size=10 * rows * width
    )(back_4[0], back_4[1], partial[0])

    product = jnp.dot(hidden_other, w_half, preferred_element_type=f32).astype(bf16)
    product_got = partner(product)
    output = (
        fwd_rows.astype(f32)
        + (jnp.dot(hidden_own, w_half, preferred_element_type=f32) + product_got.astype(f32))
    ).astype(bf16)
    passed_activation = from_behind(output[None], 1)

    (input_back,) = call(
        functools.partial(leave_kernel, rows),
        [((frames, width), bf16)],
        [VMEM] * 5,
        flops=20 * frames * width,
        size=8 * frames * width,
    )(norm_own, norm_got, saved_rows, upstream, gain)
    passed_gradient = from_behind(input_back[None], -1)
    kernel_grad, gain_grad = call(
        functools.partial(totals_kernel, rows),
        [((KW, 1, width), f32), ((1, width), f32)],
        [VMEM] * 4,
        limit=40<<20,
        flops=4 * KW * width,
        size=12 * KW * width,
    )(total, total_got, tap_rows, gain)
    (passed_gradient,) = call(
        relay_kernel, [(passed_gradient.shape, bf16)], [VMEM], size=4 * frames * width
    )(passed_gradient)
    return (
        passed_activation,
        passed_gradient,
        weight_grad[None],
        jnp.transpose(kernel_grad, (1, 0, 2)),
        gain_grad,
    )


def solution(mesh):
    sections, pieces = mesh.devices.shape
    folded = Mesh(mesh.devices.reshape(sections, pieces // 2, 2), ("section", "z", "x"))
    split = P("section", ("z", "x"), None)
    placed = (
        split,
        split,
        split,
        P("section", None),
        P("section", None, None),
        split,
        P(),
        P("section", None),
    )

    return jax.shard_map(
        per_device,
        mesh=folded,
        in_specs=placed,
        out_specs=(split, split, split, P("section", None, None), P("section", None)),
        check_vma=False,
    )
```
